256 devices in a mesh: dp: 32 (over z_lo, x, core), expert: 8 (over z_hi, y).
Axes of the slice: x: 4, y: 4, z: 8 (z_hi: 2, z_lo: 4; z = z_hi * 4 + z_lo), core: 2. Of those that a mesh axis runs over, the one named last changes fastest.
Arguments:
- acts: float32 [65536, 1024], P(('dp', 'expert')), may hold values from -18 to 18, as said below
- grads_out: float32 [65536, 1024], P(('dp', 'expert')), may hold values from -18 to 18, as said below
- routes: int32 [65536, 2], P(('dp', 'expert')), may hold values from 0 to 7, all different within a row; in each aligned block of 256 rows (0 to 255, 256 to 511, ...) at most 96 rows name the same one
- counts: int32 [256, 8], P(('dp', 'expert')), may hold values from 48 to 96
- old_act_factor: float32 [8, 1024, 1024], P('expert', 'dp'), may hold values from -1 to 4, as said below
- old_grad_factor: float32 [8, 1024, 1024], P('expert', 'dp'), may hold values from -1 to 4, as said below
- momentum: float32 [8, 1024, 1024], P('expert', 'dp'), may hold values from -0.0018 to 0.0018
- weights: float32 [8, 1024, 1024], P('expert', 'dp'), may hold values from -0.1875 to 0.1875
Outputs:
- act_factor: float32 [8, 1024, 1024], P('expert', 'dp')
- grad_factor: float32 [8, 1024, 1024], P('expert', 'dp')
- new_momentum: float32 [8, 1024, 1024], P('expert', 'dp')
- new_weights: float32 [8, 1024, 1024], P('expert', 'dp')
The draws below stay inside these ranges and needn't reach their ends.
Inputs may be any that keep to these rules, and one draw needn't show every extreme that they name: `acts`: entries are independent across rows; each feature has its own scale. `grads_out`: entries are independent across rows; each feature has its own scale. `old_act_factor`: each expert's matrix is symmetric, and each diagonal entry exceeds the sum of the magnitudes of the other entries of its row. `old_grad_factor`: each expert's matrix is symmetric, and each diagonal entry exceeds the sum of the magnitudes of the other entries of its row. `routes`: within the rows of one device no expert is named by more than 96 rows.
All inputs are finite; a program needn't handle non-finite values. Where the reference program divides by a largest or mean magnitude, that divisor is 1e-20 or more.
Results may differ from the reference program's by a relative error of at most 0.00013.
Values sent between devices are 32-bit elements; how exact they have to be, the bound alone decides.
A program may use at most 128 MiB of HBM per device.

```python
import math
import jax
import jax.numpy as jnp
import numpy as np
from jax import lax

FEAT = 1024
TOPK = 2
S_DEV = 256
EXPERTS = 8
CAP = 96
ROWS = 65536
DEVICES = 256


def feature_draw(key):
    k_scale, k_base = jax.random.split(key, 2)
    scales = jnp.exp(jax.random.uniform(k_scale, (FEAT,), jnp.float32, jnp.log(0.3), jnp.log(3.0)))
    base = jnp.clip(jax.random.normal(k_base, (ROWS, FEAT), jnp.float32), -6.0, 6.0)
    return base * scales[None, :]


def dominant_draw(key):
    k_diag, k_off = jax.random.split(key)
    diag = jnp.exp(jax.random.uniform(k_diag, (EXPERTS, FEAT), jnp.float32, 0.0, jnp.log(4.0)))
    raw = jax.random.uniform(k_off, (EXPERTS, FEAT, FEAT), jnp.float32, -1.0, 1.0) * (1.2 / FEAT)
    off = 0.5 * (raw + jnp.swapaxes(raw, 1, 2))
    unit = jnp.eye(FEAT, dtype=jnp.float32)[None, :, :]
    return off * (1.0 - unit) + diag[:, :, None] * unit


def draw_acts(key, part):
    return feature_draw(jax.random.fold_in(key, 11))


def draw_grads_out(key, part):
    return feature_draw(jax.random.fold_in(key, 23))


def draw_old_act_factor(key, part):
    return dominant_draw(jax.random.fold_in(key, 37))


def draw_old_grad_factor(key, part):
    return dominant_draw(jax.random.fold_in(key, 41))


def touch_ends(entries, stream_key, least, largest):
    index_at = [jax.random.randint(jax.random.fold_in(stream_key, axis), (), 0, length) for axis, length in enumerate(entries.shape)]
    main_axis = entries.shape.index(max(entries.shape))
    beside = index_at[:main_axis] + [(index_at[main_axis] + 1) % entries.shape[main_axis]] + index_at[main_axis + 1:]
    return entries.at[tuple(index_at)].set(least).at[tuple(beside)].set(largest)


def steps_of(stream_key, dims, cuts, smallest, high):
    def one(dim, shards_of):
        heights = jax.random.uniform(jax.random.fold_in(jax.random.fold_in(stream_key, 6), dim), (shards_of,), jnp.float32, smallest / len(cuts), high / len(cuts))
        return jnp.repeat(jnp.exp(heights), dims[dim] // shards_of).reshape((-1,) + (1,) * (len(dims) - dim - 1))

    level = one(*cuts[0])
    for cut in cuts[1:]:
        level = level * one(*cut)
    return level


def routed_block(stream_key, own, number, rows, count, top, bound, skew):
    ranking = jax.random.permutation(stream_key, count)
    packed, ordinary = portions_of(count, rows * top, bound, skew, True), portions_of(count, rows * top, bound, skew, False)
    places = jnp.arange(count)

    def named(lengths, turn):
        used = int((lengths > 0).sum())
        fixed = max(1, used // 4)
        moved = fixed + (places - fixed + turn * (used - fixed)) % max(1, count - fixed)
        return jnp.zeros((count,), jnp.int32).at[ranking[jnp.where(places < fixed, places, moved)]].set(jnp.asarray(lengths, jnp.int32))

    lengths = jnp.where(number % 4 == 0, named(packed, number // 4), named(ordinary, number - number // 4 - 1))
    mixed = jax.random.permutation(jax.random.fold_in(own, 3), count)
    donor, sink = mixed[0:count // 2 * 2:2], mixed[1:count // 2 * 2:2]
    slack = jnp.minimum(lengths[donor] - 1, bound - lengths[sink]) // 2
    slack = jnp.where((donor == ranking[0]) | (sink == ranking[0]) | (lengths[sink] == 0), 0, jnp.maximum(slack, 0))
    moved = jax.random.randint(jax.random.fold_in(own, 4), (count // 2,), 0, 1 << 20) % (slack + 1)
    lengths = lengths.at[donor].add(-moved).at[sink].add(moved)
    items = jnp.searchsorted(jnp.cumsum(lengths), jnp.arange(rows * top), side="right").astype(jnp.int32)
    table = items.reshape(top, rows).T
    table = table[jax.random.permutation(jax.random.fold_in(own, 1), rows)]
    turn = jax.random.randint(jax.random.fold_in(own, 2), (rows, 1), 0, top)
    return jnp.take_along_axis(table, (jnp.arange(top)[None, :] + turn) % top, axis=1)


def portions_of(count, total, reach, slope, full):
    loads = [(1 << 20) // math.isqrt(rank ** slope) + 1 for rank in range(1, count + 1)]
    largest = reach if full else min(reach, max(-(-total // count), total * loads[0] // sum(loads)))
    least = 1 if total - largest >= count - 1 else 0
    holding, spare = [largest] + [least] * (count - 1), total - largest - least * (count - 1)
    while spare > 0:
        movable = [i for i in range(1, count) if holding[i] < largest] or [i for i in range(1, count) if holding[i] < reach]
        whole, left = sum([loads[i] for i in movable]), spare
        for i in movable:
            extra = min(reach - holding[i], max(1, left * loads[i] // whole), spare)
            holding[i] = holding[i] + extra
            spare = spare - extra
    return np.array(holding)


def bell_draw(rng, extent, deviation, limit, pieces=(), held_as=jnp.bfloat16):
    level = steps_of(rng, extent, pieces, -0.22, 0.18) if pieces else 1.0
    drawn = jax.random.normal(rng, extent, jnp.float32) * deviation * level
    return jnp.minimum(jnp.maximum(drawn, -limit), limit).astype(held_as)


def setup_inputs(seed: int = 0) -> dict:
    seeds = jax.random.split(jax.random.key(seed), 9)
    acts = draw_acts(jax.random.fold_in(seeds[8], 71), 0)
    grads_out = draw_grads_out(jax.random.fold_in(seeds[8], 71), 0)
    routes_keys = jax.random.split(jax.random.fold_in(seeds[2], 1), ROWS // S_DEV)
    routes_turns = jax.random.permutation(jax.random.fold_in(seeds[2], 3), ROWS // S_DEV)
    routes = jax.vmap(lambda own, number: routed_block(jax.random.fold_in(seeds[2], 2), own, number, S_DEV, EXPERTS, TOPK, CAP, 2))(routes_keys, routes_turns).reshape((ROWS, TOPK))
    counts = touch_ends(jax.random.randint(seeds[3], (DEVICES, EXPERTS), CAP // 2, CAP + 1), jax.random.fold_in(seeds[3], 1), CAP // 2, CAP).astype(jnp.int32)
    old_act_factor = draw_old_act_factor(jax.random.fold_in(seeds[8], 71), 0)
    old_grad_factor = draw_old_grad_factor(jax.random.fold_in(seeds[8], 71), 0)
    momentum = bell_draw(seeds[6], (EXPERTS, FEAT, FEAT), 0.0003, 0.0018, ((0, 8), (1, 32)), jnp.float32)
    weights = bell_draw(seeds[7], (EXPERTS, FEAT, FEAT), FEAT ** -0.5, 0.1875, ((0, 8), (1, 32)), jnp.float32)
    return {"acts": acts, "grads_out": grads_out, "routes": routes, "counts": counts, "old_act_factor": old_act_factor, "old_grad_factor": old_grad_factor, "momentum": momentum, "weights": weights}


def product(left, right):
    return jnp.dot(left, right, precision=lax.Precision.HIGHEST, preferred_element_type=jnp.float32)


def damped_inverse(factor):
    size = factor.shape[0]
    unit = jnp.eye(size, dtype=jnp.float32)
    damp = 0.1 * jnp.trace(factor) / size
    shifted = factor + damp * unit
    alpha = 1.0 / jnp.max(jnp.sum(jnp.abs(shifted), axis=1))
    first = alpha * (2.0 * unit - alpha * shifted)
    return 2.0 * first - product(product(first, shifted), first)


def reference(acts, grads_out, routes, counts, old_act_factor, old_grad_factor, momentum, weights):
    rows = routes.shape[0]
    devices = rows // S_DEV
    experts = jnp.arange(EXPERTS, dtype=jnp.int32)
    hit = jnp.sum((routes[:, :, None] == experts[None, None, :]).astype(jnp.int32), axis=1, dtype=jnp.int32)
    hit_dev = hit.reshape(devices, S_DEV, EXPERTS)
    rank = jnp.cumsum(hit_dev, axis=1, dtype=jnp.int32) - hit_dev
    keep = (hit_dev * (rank < counts[:, None, :]).astype(jnp.int32)).reshape(rows, EXPERTS)
    weight = keep.astype(jnp.float32)
    total = jnp.maximum(jnp.sum(weight, axis=0), jnp.float32(1.0))

    def one_expert(item):
        column, count, old_a, old_g, moment, current = item
        kept_acts = acts * column[:, None]
        kept_grads = grads_out * column[:, None]
        act_stat = product(kept_acts.T, kept_acts) / count
        grad_stat = product(kept_grads.T, kept_grads) / count
        gradient = product(kept_grads.T, kept_acts) / count
        act_new = 0.5 * old_a + 0.5 * act_stat
        grad_new = 0.5 * old_g + 0.5 * grad_stat
        precond = product(product(damped_inverse(grad_new), gradient), damped_inverse(act_new))
        moment_new = 0.9 * moment + precond
        return act_new, grad_new, moment_new, current - 0.5 * moment_new

    act_factor, grad_factor, new_momentum, new_weights = lax.map(
        one_expert, (weight.T, total, old_act_factor, old_grad_factor, momentum, weights))
    return (act_factor, grad_factor, new_momentum, new_weights)
```

```python
import jax
import jax.numpy as jnp
from jax import lax
from jax.experimental import pallas as pl
from jax.experimental.pallas import tpu as pltpu
from jax.sharding import PartitionSpec as P

MESH = pl.DeviceIdType.MESH
F32 = jnp.float32
BF16 = jnp.bfloat16
ROWS = 256
FEAT = 1024
CAP = 96
WIN = 640
EXT = 1536
SUM_COLS = ((0, 768), (768, 640), (1408, 1024))
SUM_W = 2432
ALL_COLS = ((0, 640), (640, 640), (1280, 1024))
ALL_W = 2304


def coords():
    dp = lax.axis_index("dp")
    ex = lax.axis_index("expert")
    c = lax.rem(dp, 2)
    x = lax.rem(lax.div(dp, 2), 4)
    zl = lax.div(dp, 8)
    y = lax.rem(ex, 4)
    zh = lax.div(ex, 4)
    return x, y, zl, zh, c


def device(x, y, z, c):
    return (lax.rem(z, 4) * 8 + x * 2 + c, lax.div(z, 4) * 4 + y)


def remote(src, dst, send, recv, dev):
    return pltpu.make_async_remote_copy(
        src_ref=src, dst_ref=dst, send_sem=send, recv_sem=recv, device_id=dev, device_id_type=MESH
    )


def dot(a, b):
    return jnp.dot(a, b, preferred_element_type=F32)


def dot_t(a, b):
    return lax.dot_general(a, b, (((0,), (0,)), ((), ())), preferred_element_type=F32)


def split(v):
    hi = v.astype(BF16)
    return hi, (v - hi.astype(F32)).astype(BF16)


def gather_kernel(
    acts, grads, pos, out, raw_a, raw_g, posb, pkh, pkl,
    loc, s_y, r_y, s_f, r_f, s_p, r_p, s_q, r_q,
):
    x, y, zl, zh, c = coords()
    z = zh * 4 + zl
    up, down, far = lax.rem(y + 1, 4), lax.rem(y + 3, 4), lax.rem(y + 2, 4)
    d_up, d_down, d_mate = device(x, up, z, c), device(x, down, z, c), device(x, y, z, 1 - c)
    peers = [
        d_up, d_down, device(x, far, z, c), d_mate,
        device(x, up, z, 1 - c), device(x, down, z, 1 - c), device(x, far, z, 1 - c),
    ]
    barrier = pltpu.get_barrier_semaphore()
    for peer in peers:
        pl.semaphore_signal(barrier, inc=1, device_id=peer, device_id_type=MESH)
    pl.semaphore_wait(barrier, 7)

    src = (acts, grads)
    raw = (raw_a, raw_g)

    def piece(t, slot, half):
        return raw[t].at[pl.ds(slot * ROWS + half * 128, 128), :]

    def own(t, half):
        return src[t].at[pl.ds(half * 128, 128), :]

    started = []

    def go(cp):
        cp.start()
        started.append(cp)

    locals_ = [
        pltpu.make_async_copy(src[t], raw[t].at[pl.ds(0, ROWS), :], loc.at[t]) for t in range(2)
    ]
    locals_.append(pltpu.make_async_copy(pos, posb.at[0], loc.at[2]))
    for cp in locals_:
        cp.start()
    toward = (d_up, d_down)
    direct, forward, mate = {}, {}, {}
    for t in range(2):
        for turn in range(2):
            for way in range(2):
                half = turn ^ way
                direct[way, t, half] = remote(
                    own(t, half), piece(t, 1 + way, half), s_y.at[way, t, half],
                    r_y.at[way, t, half], toward[way],
                )
                go(direct[way, t, half])
        for half in range(2):
            mate[0, t, half] = remote(
                own(t, half), piece(t, 4, half), s_p.at[0, t, half], r_p.at[0, t, half], d_mate
            )
            go(mate[0, t, half])
        if t == 0:
            quick = []
            for i, peer in enumerate(peers):
                quick.append(
                    remote(pos, posb.at[i + 1], s_q.at[i + 1], r_q.at[i + 1], peer)
                )
                go(quick[-1])

    def relay(slot, t, half):
        mate[slot, t, half] = remote(
            piece(t, slot, half), piece(t, 4 + slot, half), s_p.at[slot, t, half],
            r_p.at[slot, t, half], d_mate,
        )
        go(mate[slot, t, half])

    lane = c * 4 + y
    slot_ids = lax.broadcasted_iota(jnp.int32, (CAP, ROWS), 0)

    def pack(t):
        def body(s, carry):
            row = posb[s, pl.ds(lane, 1), :]
            sel = jnp.where(slot_ids == row, F32(1.0), F32(0.0)).astype(BF16)
            at = pl.ds(pl.multiple_of(s * CAP, CAP), CAP)
            for cb in range(4):
                v = raw[t][pl.ds(pl.multiple_of(s * ROWS, ROWS), ROWS), cb * 256:(cb + 1) * 256]
                hi, lo = split(v)
                for part, dest in ((hi, pkh), (lo, pkl)):
                    got = dot(sel, part).astype(BF16)
                    base = t * EXT + cb * 256
                    dest[at, base:base + 256] = got
                    if cb < 2:
                        dest[at, base + FEAT:base + FEAT + 256] = got
            return carry

        lax.fori_loop(0, 8, body, 0)

    def gram(lhs, rhs, width, store):
        def body(ib, carry):
            at = pl.multiple_of(ib * 256, 256)
            lh = pkh[:, pl.ds(lhs + at, 256)]
            ll = pkl[:, pl.ds(lhs + at, 256)]
            for nb in range(width // 256):
                begin = rhs(at) + nb * 256
                rh = pkh[:, pl.ds(begin, 256)]
                rl = pkl[:, pl.ds(begin, 256)]
                store(at, nb, dot_t(lh, rh) + (dot_t(lh, rl) + dot_t(ll, rh)))
            return carry

        lax.fori_loop(0, 4, body, 0)

    def window_store(first):
        def store(at, nb, acc):
            top, bottom = pl.ds(at, 128), pl.ds(at + 128, 128)
            lo, hi = nb * 256, nb * 256 + 256
            keep = min(hi, WIN)
            out[top, first + lo:first + keep] = acc[:128, :keep - lo]
            begin = max(lo - 128, 0)
            out[bottom, first + begin:first + hi - 128] = acc[128:, begin + 128 - lo:]
        return store

    def cross_store(at, nb, acc):
        out[pl.ds(at, 256), 1408 + nb * 256:1408 + nb * 256 + 256] = acc

    for cp in locals_:
        cp.wait()
    for t in range(2):
        for turn in range(2):
            for way in range(2):
                half = turn ^ way
                direct[way, t, half].wait_recv()
                if turn == 0:
                    forward[way, t] = remote(
                        piece(t, 1 + way, half), piece(t, 3, half), s_f.at[way, t],
                        r_f.at[way, t], toward[way],
                    )
                    go(forward[way, t])
                relay(1 + way, t, half)
        for way in range(2):
            forward[way, t].wait_recv()
            relay(3, t, way)
        if t == 0:
            for cp in quick:
                cp.wait_recv()
            held = jnp.zeros((8, ROWS), F32)
            for s in range(8):
                row = posb[s, pl.ds(lane, 1), :]
                held = held + jnp.where(row >= 0, F32(1.0), F32(0.0))
            count = jnp.sum(held[0:1, :])
            out[:, 640:768] = jnp.full((FEAT, 128), count, F32)
        for slot in range(4):
            for half in range(2):
                mate[slot, t, half].wait_recv()
        pack(t)
        gram(t * EXT, lambda at, t=t: t * EXT + at, 768, window_store(SUM_COLS[t][0]))
    gram(EXT, lambda at: 0, FEAT, cross_store)
    for cp in started:
        cp.wait_send()


def reduce_kernel(
    part, old_a, old_g, mom, wts, out_a, out_g, out_m, out_w,
    x1, x2a, x2b, acc, z4p, z4m, zp, zm, fin, shard, full, ext, fac, mh, ml,
    s_x, r_x, s_z, r_z, s_c, r_c, s_gz, r_gz, s_gx, r_gx, s_gc, r_gc,
):
    x, y, zl, zh, c = coords()
    z = zh * 4 + zl
    right, left, opp = lax.rem(x + 1, 4), lax.rem(x + 3, 4), lax.rem(x + 2, 4)
    d_right, d_left = device(right, y, z, c), device(left, y, z, c)
    d_up, d_down = device(x, y, lax.rem(z + 1, 8), c), device(x, y, lax.rem(z + 7, 8), c)
    d_mate = device(x, y, z, 1 - c)
    barrier = pltpu.get_barrier_semaphore()
    for peer in (d_right, d_left, d_up, d_down, d_mate):
        pl.semaphore_signal(barrier, inc=1, device_id=peer, device_id_type=MESH)
    pl.semaphore_wait(barrier, 5)

    home = zh == c
    sides = (d_right, d_left)
    near = (right, left)
    lo_half, hi_half = pl.ds(0, 32), pl.ds(32, 32)
    trav, rest = (lo_half, hi_half), (hi_half, lo_half)

    def cols(p):
        return pl.ds(SUM_COLS[p][0], SUM_COLS[p][1])

    def copy_x(p, way, kind):
        if kind == 0:
            s, d = part.at[:, opp, trav[way], cols(p)], x1.at[way, :, :, cols(p)]
        elif kind == 1:
            s, d = part.at[:, near[way], rest[way], cols(p)], x2b.at[way, :, :, cols(p)]
        else:
            s, d = x1.at[way, :, :, cols(p)], x2a.at[way, :, :, cols(p)]
        return remote(s, d, s_x.at[p, way, kind], r_x.at[p, way, kind], sides[way])

    def x_send(p, kind):
        for way in range(2):
            copy_x(p, way, kind).start()

    def x_relay(p):
        for way in range(2):
            copy_x(p, way, 0).wait_recv()

            def body(b, carry):
                x1[way, b, :, cols(p)] = x1[way, b, :, cols(p)] + part[b, near[way], trav[way], cols(p)]
                return carry

            lax.fori_loop(0, 4, body, 0)
        x_send(p, 2)

    def x_final(p):
        for way in range(2):
            copy_x(p, way, 1).wait_recv()
            copy_x(p, way, 2).wait_recv()

        def body(b, carry):
            acc[b, lo_half, cols(p)] = part[b, x, lo_half, cols(p)] + (
                x2a[0, b, :, cols(p)] + x2b[1, b, :, cols(p)])
            acc[b, hi_half, cols(p)] = part[b, x, hi_half, cols(p)] + (
                x2a[1, b, :, cols(p)] + x2b[0, b, :, cols(p)])
            return carry

        lax.fori_loop(0, 4, body, 0)

    z_sides = (d_up, d_down)
    z4 = (z4p, z4m)
    zz = (zp, zm)

    def target(way, k):
        zd = lax.rem(z + k, 8) if way == 0 else lax.rem(z + 8 - k, 8)
        return lax.rem(zd, 4), lax.div(zd, 4) == c

    def copy_z(p, way, kind):
        k = (4, 3, 3, 2, 1)[kind]
        b, _ = target(way, k)
        if kind == 0:
            s, d = acc.at[b, trav[way], cols(p)], z4[way].at[:, cols(p)]
        elif kind == 1:
            s, d = z4[way].at[:, cols(p)], zz[way].at[0, trav[way], cols(p)]
        elif kind == 2:
            s, d = acc.at[b, rest[way], cols(p)], zz[way].at[0, rest[way], cols(p)]
        elif kind == 3:
            s, d = zz[way].at[0, :, cols(p)], zz[way].at[1, :, cols(p)]
        else:
            s, d = zz[way].at[1, :, cols(p)], zz[way].at[2, :, cols(p)]
        return remote(s, d, s_z.at[p, way, kind], r_z.at[p, way, kind], z_sides[way])

    def z_first(p):
        for way in range(2):
            @pl.when(target(way, 4)[1])
            def _(way=way):
                copy_z(p, way, 0).start()

            @pl.when(target(way, 3)[1])
            def _(way=way):
                copy_z(p, way, 2).start()

    def z_step(p, k):
        for way in range(2):
            @pl.when(target(way, k)[1])
            def _(way=way):
                b, _ = target(way, k)
                if k == 3:
                    copy_z(p, way, 0).wait_recv()
                    z4[way][:, cols(p)] = z4[way][:, cols(p)] + acc[b, trav[way], cols(p)]
                    copy_z(p, way, 1).start()
                else:
                    got = 2 - k
                    if k == 2:
                        copy_z(p, way, 1).wait_recv()
                        copy_z(p, way, 2).wait_recv()
                    else:
                        copy_z(p, way, 3).wait_recv()
                    zz[way][got, :, cols(p)] = zz[way][got, :, cols(p)] + acc[b, :, cols(p)]
                    copy_z(p, way, 5 - k).start()

    def copy_c(p):
        return remote(
            acc.at[zl, pl.ds((1 - c) * 32, 32), cols(p)], fin.at[:, cols(p)], s_c.at[p], r_c.at[p], d_mate
        )

    def z_final(p):
        @pl.when(home)
        def _():
            copy_z(p, 0, 4).wait_recv()
            copy_z(p, 1, 4).wait_recv()
            acc[zl, :, cols(p)] = acc[zl, :, cols(p)] + (zp[2, :, cols(p)] + zm[2, :, cols(p)])
            copy_c(p).start()
            fin[:, cols(p)] = acc[zl, pl.ds(c * 32, 32), cols(p)]

    olds = (old_a, old_g)
    block = zl * 2 + lax.div(x, 2)

    def make_shard(p):
        @pl.when(jnp.logical_not(home))
        def _():
            copy_c(p).wait_recv()
        total = jnp.maximum(fin[0:1, 640:641], F32(1.0))
        at = ALL_COLS[p]
        if p < 2:
            ext[:, 0:FEAT] = olds[p][0]
            ext[:, FEAT:EXT] = olds[p][0, :, 0:EXT - FEAT]
            old = ext[:, pl.ds(pl.multiple_of(block * 128, 128), WIN)]
            begin = SUM_COLS[p][0]
            shard[:, at[0]:at[0] + WIN] = 0.5 * old + 0.5 * (fin[:, begin:begin + WIN] / total)
        else:
            begin = SUM_COLS[p][0]
            shard[:, at[0]:at[0] + FEAT] = fin[:, begin:begin + FEAT] / total
        full[zl, x, c, :, at[0]:at[0] + at[1]] = shard[:, at[0]:at[0] + at[1]]

    def acols(p):
        return pl.ds(ALL_COLS[p][0], ALL_COLS[p][1])

    def copy_gz(p, way, step):
        origin = zl - (step - 1) if way == 0 else zl + (step - 1)
        ok = jnp.logical_and(origin >= 0, zl < 3) if way == 0 else jnp.logical_and(origin <= 3, zl > 0)
        ref = full.at[jnp.clip(origin, 0, 3), x, c, :, acols(p)]
        s = shard.at[:, acols(p)] if step == 1 else ref
        return ok, remote(s, ref, s_gz.at[p, way, step - 1], r_gz.at[p, way, step - 1], z_sides[way])

    def gz_send(p, step):
        for way in range(2):
            ok, cp = copy_gz(p, way, step)
            @pl.when(ok)
            def _(cp=cp):
                cp.start()

    def gz_wait(p, step):
        for way in range(2):
            ok = zl - step >= 0 if way == 0 else zl + step <= 3
            cp = copy_gz(p, way, step)[1]
            @pl.when(ok)
            def _(cp=cp):
                cp.wait_recv()

    def copy_gx(p, way, kind):
        if kind == 0:
            ref = full.at[:, x, c, :, acols(p)]
        else:
            who = left if way == 0 else right
            ref = full.at[:, who, c, pl.ds(16 * way, 16), acols(p)]
        return remote(ref, ref, s_gx.at[p, way, kind], r_gx.at[p, way, kind], sides[way])

    def copy_gc(p, i):
        who = (x, left, right, opp)[i]
        ref = full.at[:, who, c, :, acols(p)]
        return remote(ref, ref, s_gc.at[p, i], r_gc.at[p, i], d_mate)

    def gx_send(p):
        for way in range(2):
            copy_gx(p, way, 0).start()
        copy_gc(p, 0).start()

    def gx_forward(p):
        for way in range(2):
            copy_gx(p, way, 0).wait_recv()
            copy_gx(p, way, 1).start()
            copy_gc(p, 1 + way).start()

    def gx_last(p):
        for way in range(2):
            copy_gx(p, way, 1).wait_recv()
        copy_gc(p, 3).start()

    def g_wait(p):
        for i in range(4):
            copy_gc(p, i).wait_recv()

    x_send(0, 0)
    x_send(0, 1)
    x_send(1, 0)
    x_relay(0)
    x_send(1, 1)
    x_send(2, 0)
    x_relay(1)
    x_final(0)
    z_first(0)
    x_send(2, 1)
    x_relay(2)
    z_step(0, 3)
    x_final(1)
    z_first(1)
    z_step(0, 2)
    z_step(1, 3)
    z_step(0, 1)
    x_final(2)
    z_first(2)
    z_step(1, 2)
    z_final(0)
    z_step(2, 3)
    z_step(1, 1)
    make_shard(0)
    gz_send(0, 1)
    z_step(2, 2)
    z_final(1)
    z_step(2, 1)
    gz_wait(0, 1)
    gz_send(0, 2)
    make_shard(1)
    gz_send(1, 1)
    z_final(2)
    gz_wait(0, 2)
    gz_send(0, 3)
    make_shard(2)
    gz_send(2, 1)
    gz_wait(1, 1)
    gz_send(1, 2)
    gz_wait(0, 3)
    gx_send(0)
    gz_wait(2, 1)
    gz_send(2, 2)
    gz_wait(1, 2)
    gz_send(1, 3)
    gz_wait(2, 2)
    gz_send(2, 3)
    gz_wait(1, 3)
    gx_forward(0)
    gx_send(1)
    gz_wait(2, 3)
    gx_last(0)
    gx_forward(1)
    gx_send(2)
    gx_last(1)
    gx_forward(2)

    row_ids = lax.broadcasted_iota(jnp.int32, (128, FEAT), 0)
    col_ids = lax.broadcasted_iota(jnp.int32, (128, FEAT), 1)
    alphas, damps = [], []
    for t in range(2):
        g_wait(t)
        first = ALL_COLS[t][0]

        def rows_of(i, first_col):
            b, h = lax.div(i, 2), lax.rem(i, 2)
            got = full[b, pl.ds(h * 2, 2), :, :, first_col]
            return got.reshape(128, 128)

        def build(i, tr, t=t, first=first):
            at = pl.ds(pl.multiple_of(i * 128, 128), 128)
            for k in range(8):
                j = lax.rem(i + k, 8)
                if k <= 4:
                    blk = rows_of(i, pl.ds(first + k * 128, 128))
                else:
                    blk = rows_of(j, pl.ds(first + (8 - k) * 128, 128)).T
                if k == 0:
                    tr = tr + jnp.sum(jnp.where(row_ids[:, :128] == col_ids[:, :128], blk, F32(0.0)))
                fac[t, at, pl.ds(pl.multiple_of(j * 128, 128), 128)] = blk
            return tr

        trace = lax.fori_loop(0, 8, build, F32(0.0))
        damp = F32(0.1) * trace / F32(FEAT)

        def shift(i, best, t=t, damp=damp):
            at = pl.ds(pl.multiple_of(i * 128, 128), 128)
            m = fac[t, at, :] + jnp.where(row_ids + i * 128 == col_ids, damp, F32(0.0))
            hi, lo = split(m)
            mh[t, at, :] = hi
            ml[t, at, :] = lo
            return jnp.maximum(best, jnp.max(jnp.sum(jnp.abs(m), axis=1, keepdims=True)))

        best = lax.fori_loop(0, 8, shift, F32(0.0))
        alphas.append(F32(1.0) / jnp.full((1, 1), best, F32))
        damps.append(damp)
        if t == 0:
            gx_last(2)

    d = zl * 8 + x * 2 + c
    mine = pl.ds(pl.multiple_of(d * 32, 32), 32)
    out_a[0] = fac[0, mine, :]
    out_g[0] = fac[1, mine, :]

    def times(v, t):
        hi, lo = split(v)
        both = jnp.concatenate([hi, lo], axis=0)
        parts = []
        for nb in range(4):
            at = slice(nb * 256, nb * 256 + 256)
            one = dot(both, mh[t, :, at])
            parts.append(one[:32] + (one[32:] + dot(hi, ml[t, :, at])))
        return jnp.concatenate(parts, axis=1)

    aa, ag = alphas
    unit_rows = jnp.where(
        lax.broadcasted_iota(jnp.int32, (32, FEAT), 0) + d * 32
        == lax.broadcasted_iota(jnp.int32, (32, FEAT), 1), F32(1.0), F32(0.0))
    shifted_rows = fac[1, mine, :] + damps[1] * unit_rows
    u1 = ag * (2.0 * unit_rows - ag * shifted_rows)
    u2 = times(u1, 1)
    inv_rows = 2.0 * u1 - ag * (2.0 * u2 - ag * times(u2, 1))
    g_wait(2)
    hi, lo = split(inv_rows)
    both = jnp.concatenate([hi, lo], axis=0)
    parts = []
    for nb in range(4):
        rh, rl = split(full[:, :, :, :, 1280 + nb * 256:1536 + nb * 256].reshape(FEAT, 256))
        one = dot(both, rh)
        parts.append(one[:32] + (one[32:] + dot(hi, rl)))
    lhs = jnp.concatenate(parts, axis=1)
    half_way = aa * (2.0 * lhs - aa * times(lhs, 0))
    w = times(half_way, 0)
    precond = 2.0 * half_way - aa * (2.0 * w - aa * times(w, 0))
    moment = 0.9 * mom[0] + precond
    out_m[0] = moment
    out_w[0] = wts[0] - 0.5 * moment

    for p in range(3):
        for way in range(2):
            for kind in range(3):
                copy_x(p, way, kind).wait_send()
            for kind in range(5):
                k = (4, 3, 3, 2, 1)[kind]
                @pl.when(target(way, k)[1])
                def _(p=p, way=way, kind=kind):
                    copy_z(p, way, kind).wait_send()
            for step in range(1, 4):
                ok, cp = copy_gz(p, way, step)
                @pl.when(ok)
                def _(cp=cp):
                    cp.wait_send()
            for kind in range(2):
                copy_gx(p, way, kind).wait_send()
        @pl.when(home)
        def _(p=p):
            copy_c(p).wait_send()
        for i in range(4):
            copy_gc(p, i).wait_send()


def on_device(acts, grads_out, routes, counts, old_act_factor, old_grad_factor, momentum, weights):
    experts = jnp.arange(8, dtype=jnp.int32)
    hit = jnp.sum(
        (routes.T[:, None, :] == experts[None, :, None]).astype(jnp.int32), axis=0, dtype=jnp.int32
    )
    rank = jnp.cumsum(hit, axis=1, dtype=jnp.int32) - hit
    kept = (hit > 0) & (rank < counts[0][:, None])
    pos = jnp.where(kept, rank, -1)
    vm = pl.BlockSpec(memory_space=pltpu.VMEM)
    hbm = pl.BlockSpec(memory_space=pl.ANY)
    dma = pltpu.SemaphoreType.DMA
    sums = pl.pallas_call(
        gather_kernel,
        out_shape=jax.ShapeDtypeStruct((FEAT, SUM_W), F32),
        in_specs=[hbm, hbm, hbm],
        out_specs=vm,
        scratch_shapes=[
            pltpu.VMEM((8 * ROWS, FEAT), F32),
            pltpu.VMEM((8 * ROWS, FEAT), F32),
            pltpu.VMEM((8, 8, ROWS), jnp.int32),
            pltpu.VMEM((8 * CAP, 2 * EXT), BF16),
            pltpu.VMEM((8 * CAP, 2 * EXT), BF16),
            dma((3,)), dma((2, 2, 2)), dma((2, 2, 2)), dma((2, 2)), dma((2, 2)),
            dma((4, 2, 2)), dma((4, 2, 2)), dma((8,)), dma((8,)),
        ],
        compiler_params=pltpu.CompilerParams(
            collective_id=0, has_side_effects=True, vmem_limit_bytes=60 * 1024 * 1024
        ),
        name="gather_rows",
    )(acts, grads_out, pos)
    out = jax.ShapeDtypeStruct((1, 32, FEAT), F32)
    return pl.pallas_call(
        reduce_kernel,
        out_shape=(out, out, out, out),
        in_specs=[vm] * 5,
        out_specs=[vm] * 4,
        scratch_shapes=[
            pltpu.VMEM((2, 4, 32, SUM_W), F32),
            pltpu.VMEM((2, 4, 32, SUM_W), F32),
            pltpu.VMEM((2, 4, 32, SUM_W), F32),
            pltpu.VMEM((4, 64, SUM_W), F32),
            pltpu.VMEM((32, SUM_W), F32),
            pltpu.VMEM((32, SUM_W), F32),
            pltpu.VMEM((3, 64, SUM_W), F32),
            pltpu.VMEM((3, 64, SUM_W), F32),
            pltpu.VMEM((32, SUM_W), F32),
            pltpu.VMEM((32, ALL_W), F32),
            pltpu.VMEM((4, 4, 2, 32, ALL_W), F32),
            pltpu.VMEM((32, EXT), F32),
            pltpu.VMEM((2, FEAT, FEAT), F32),
            pltpu.VMEM((2, FEAT, FEAT), BF16),
            pltpu.VMEM((2, FEAT, FEAT), BF16),
            dma((3, 2, 3)), dma((3, 2, 3)), dma((3, 2, 5)), dma((3, 2, 5)), dma((3,)), dma((3,)),
            dma((3, 2, 3)), dma((3, 2, 3)), dma((3, 2, 2)), dma((3, 2, 2)), dma((3, 4)), dma((3, 4)),
        ],
        compiler_params=pltpu.CompilerParams(
            collective_id=1, has_side_effects=True, vmem_limit_bytes=63 * 1024 * 1024
        ),
        name="reduce_apply",
    )(sums.reshape(4, 4, 64, SUM_W), old_act_factor, old_grad_factor, momentum, weights)


def solution(mesh):
    rows = P(("dp", "expert"), None)
    mats = P("expert", "dp", None)
    return jax.shard_map(
        on_device,
        mesh=mesh,
        in_specs=(rows, rows, rows, rows, mats, mats, mats, mats),
        out_specs=(mats, mats, mats, mats),
        check_vma=False,
    )
```

```python
import jax
import jax.numpy as jnp
from jax import lax
from jax.experimental import pallas as pl
from jax.experimental.pallas import tpu as pltpu
from jax.sharding import PartitionSpec as P

MESH = pl.DeviceIdType.MESH
F32 = jnp.float32
BF16 = jnp.bfloat16
ROWS = 256
FEAT = 1024
CAP = 96
SLOTS = 8 * CAP
WIN = 640
EXT = 1536
SUM_COLS = ((0, 768), (768, 640), (1408, 1024))
SUM_W = 2432
ALL_COLS = ((0, 640), (640, 640), (1280, 1024))
ALL_W = 2304


def coords():
    dp = lax.axis_index("dp")
    ex = lax.axis_index("expert")
    c = lax.rem(dp, 2)
    x = lax.rem(lax.div(dp, 2), 4)
    zl = lax.div(dp, 8)
    y = lax.rem(ex, 4)
    zh = lax.div(ex, 4)
    return x, y, zl, zh, c


def device(x, y, z, c):
    return (lax.rem(z, 4) * 8 + x * 2 + c, lax.div(z, 4) * 4 + y)


def remote(src, dst, send, recv, dev):
    return pltpu.make_async_remote_copy(
        src_ref=src, dst_ref=dst, send_sem=send, recv_sem=recv, device_id=dev, device_id_type=MESH
    )


def dot(a, b):
    return jnp.dot(a, b, preferred_element_type=F32)


def dot_t(a, b):
    return lax.dot_general(a, b, (((0,), (0,)), ((), ())), preferred_element_type=F32)


def split(v):
    hi = v.astype(BF16)
    return hi, (v - hi.astype(F32)).astype(BF16)


def step_kernel(
    acts, grads, pos, old_a, old_g, out,
    raw_a, raw_g, posb, pkh, pkl, part,
    x1, x2a, x2b, z4p, z4m, zp, zm, fin, full, ext,
    loc, s_y, r_y, s_f, r_f, s_p, r_p, s_q, r_q,
    s_x, r_x, s_z, r_z, s_c, r_c, s_gz, r_gz, s_gx, r_gx, s_gc, r_gc,
):
    x, y, zl, zh, c = coords()
    z = zh * 4 + zl
    right, left, opp = lax.rem(x + 1, 4), lax.rem(x + 3, 4), lax.rem(x + 2, 4)
    d_right, d_left = device(right, y, z, c), device(left, y, z, c)
    d_ztop, d_zlow = device(x, y, lax.rem(z + 1, 8), c), device(x, y, lax.rem(z + 7, 8), c)
    up, down, far = lax.rem(y + 1, 4), lax.rem(y + 3, 4), lax.rem(y + 2, 4)
    d_up, d_down, d_mate = device(x, up, z, c), device(x, down, z, c), device(x, y, z, 1 - c)
    peers = [
        d_up, d_down, device(x, far, z, c), d_mate,
        device(x, up, z, 1 - c), device(x, down, z, 1 - c), device(x, far, z, 1 - c),
    ]
    barrier = pltpu.get_barrier_semaphore()
    for peer in peers + [d_right, d_left, d_ztop, d_zlow]:
        pl.semaphore_signal(barrier, inc=1, device_id=peer, device_id_type=MESH)
    pl.semaphore_wait(barrier, 11)

    src = (acts, grads)
    raw = (raw_a, raw_g)

    def piece(t, slot, half):
        return raw[t].at[pl.ds(slot * ROWS + half * 128, 128), :]

    def own(t, half):
        return src[t].at[pl.ds(half * 128, 128), :]

    started = []

    def go(cp):
        cp.start()
        started.append(cp)

    locals_ = [
        pltpu.make_async_copy(src[t], raw[t].at[pl.ds(0, ROWS), :], loc.at[t]) for t in range(2)
    ]
    locals_.append(pltpu.make_async_copy(pos, posb.at[0], loc.at[2]))
    for cp in locals_:
        cp.start()
    toward = (d_up, d_down)
    direct, forward, mate = {}, {}, {}

    def send_rows(t):
        for turn in range(2):
            for way in range(2):
                half = turn ^ way
                direct[way, t, half] = remote(
                    own(t, half), piece(t, 1 + way, half), s_y.at[way, t, half],
                    r_y.at[way, t, half], toward[way],
                )
                go(direct[way, t, half])
        for half in range(2):
            mate[0, t, half] = remote(
                own(t, half), piece(t, 4, half), s_p.at[0, t, half], r_p.at[0, t, half], d_mate
            )
            go(mate[0, t, half])

    send_rows(0)
    quick = []
    for i, peer in enumerate(peers):
        quick.append(remote(pos, posb.at[i + 1], s_q.at[i + 1], r_q.at[i + 1], peer))
        go(quick[-1])

    def relay(slot, t, half):
        mate[slot, t, half] = remote(
            piece(t, slot, half), piece(t, 4 + slot, half), s_p.at[slot, t, half],
            r_p.at[slot, t, half], d_mate,
        )
        go(mate[slot, t, half])

    lane = c * 4 + y
    slot_ids = lax.broadcasted_iota(jnp.int32, (CAP, ROWS), 0)

    def pack(t):
        def body(s, carry):
            row = posb[s, pl.ds(lane, 1), :]
            sel = jnp.where(slot_ids == row, F32(1.0), F32(0.0)).astype(BF16)
            at = pl.ds(pl.multiple_of(s * CAP, CAP), CAP)
            for cb in range(4):
                v = raw[t][pl.ds(pl.multiple_of(s * ROWS, ROWS), ROWS), cb * 256:(cb + 1) * 256]
                hi, lo = split(v)
                for part, dest in ((hi, pkh), (lo, pkl)):
                    got = dot(sel, part).astype(BF16)
                    base = t * EXT + cb * 256
                    dest[at, base:base + 256] = got
                    if cb < 2:
                        dest[at, base + FEAT:base + FEAT + 256] = got
            return carry

        lax.fori_loop(0, 8, body, 0)

    def gram(lhs, rhs, width, store, begin_block, end_block):
        def body(ib, carry):
            at = pl.multiple_of(ib * 256, 256)
            lh = pkh[:, pl.ds(lhs + at, 256)]
            ll = pkl[:, pl.ds(lhs + at, 256)]
            for nb in range(width // 256):
                begin = rhs(at) + nb * 256
                rh = pkh[:, pl.ds(begin, 256)]
                rl = pkl[:, pl.ds(begin, 256)]
                store(ib, nb, dot_t(lh, rh) + (dot_t(lh, rl) + dot_t(ll, rh)))
            return carry

        lax.fori_loop(begin_block, end_block, body, 0)

    def window_store(first):
        def store(ib, nb, got):
            lo, hi = nb * 256, nb * 256 + 256
            keep = min(hi, WIN)
            part[ib, 0:2, :, first + lo:first + keep] = got[:128, :keep - lo].reshape(2, 64, keep - lo)
            begin = max(lo - 128, 0)
            part[ib, 2:4, :, first + begin:first + hi - 128] = got[128:, begin + 128 - lo:].reshape(
                2, 64, hi - 128 - begin)
        return store

    def cross_store(ib, nb, got):
        part[ib, :, :, 1408 + nb * 256:1408 + nb * 256 + 256] = got.reshape(4, 64, 256)

    def factor_gram(t, begin_block, end_block):
        gram(t * EXT, lambda at: t * EXT + at, 768, window_store(SUM_COLS[t][0]), begin_block, end_block)

    def cross_gram(begin_block, end_block):
        gram(EXT, lambda at: 0, FEAT, cross_store, begin_block, end_block)

    def first_rows(t):
        for way in range(2):
            direct[way, t, way].wait_recv()
            forward[way, t] = remote(
                piece(t, 1 + way, way), piece(t, 3, way), s_f.at[way, t], r_f.at[way, t], toward[way]
            )
            go(forward[way, t])
            relay(1 + way, t, way)

    def second_rows(t):
        for way in range(2):
            direct[way, t, 1 - way].wait_recv()
            relay(1 + way, t, 1 - way)

    def last_rows(t):
        for way in range(2):
            forward[way, t].wait_recv()
            relay(3, t, way)

    def mate_rows(t):
        for slot in range(4):
            for half in range(2):
                mate[slot, t, half].wait_recv()

    home = zh == c
    sides = (d_right, d_left)
    near = (right, left)
    lo_half, hi_half = pl.ds(0, 32), pl.ds(32, 32)
    trav, rest = (lo_half, hi_half), (hi_half, lo_half)

    def cols(p):
        return pl.ds(SUM_COLS[p][0], SUM_COLS[p][1])

    def copy_x(p, way, kind):
        if kind == 0:
            s, d = part.at[:, opp, trav[way], cols(p)], x1.at[way, :, :, cols(p)]
        elif kind == 1:
            s, d = part.at[:, near[way], rest[way], cols(p)], x2b.at[way, :, :, cols(p)]
        else:
            s, d = x1.at[way, :, :, cols(p)], x2a.at[way, :, :, cols(p)]
        return remote(s, d, s_x.at[p, way, kind], r_x.at[p, way, kind], sides[way])

    def x_send(p, kind):
        for way in range(2):
            copy_x(p, way, kind).start()

    def x_relay(p):
        for way in range(2):
            copy_x(p, way, 0).wait_recv()

            def body(b, carry):
                x1[way, b, :, cols(p)] = x1[way, b, :, cols(p)] + part[b, near[way], trav[way], cols(p)]
                return carry

            lax.fori_loop(0, 4, body, 0)
        x_send(p, 2)

    def x_final(p):
        for way in range(2):
            copy_x(p, way, 1).wait_recv()
            copy_x(p, way, 2).wait_recv()

        def body(b, carry):
            part[b, x, lo_half, cols(p)] = part[b, x, lo_half, cols(p)] + (
                x2a[0, b, :, cols(p)] + x2b[1, b, :, cols(p)])
            part[b, x, hi_half, cols(p)] = part[b, x, hi_half, cols(p)] + (
                x2a[1, b, :, cols(p)] + x2b[0, b, :, cols(p)])
            return carry

        lax.fori_loop(0, 4, body, 0)

    z_sides = (d_ztop, d_zlow)
    z4 = (z4p, z4m)
    zz = (zp, zm)

    def target(way, k):
        zd = lax.rem(z + k, 8) if way == 0 else lax.rem(z + 8 - k, 8)
        return lax.rem(zd, 4), lax.div(zd, 4) == c

    def copy_z(p, way, kind):
        k = (4, 3, 3, 2, 1)[kind]
        b, _ = target(way, k)
        if kind == 0:
            s, d = part.at[b, x, trav[way], cols(p)], z4[way].at[:, cols(p)]
        elif kind == 1:
            s, d = z4[way].at[:, cols(p)], zz[way].at[0, trav[way], cols(p)]
        elif kind == 2:
            s, d = part.at[b, x, rest[way], cols(p)], zz[way].at[0, rest[way], cols(p)]
        elif kind == 3:
            s, d = zz[way].at[0, :, cols(p)], zz[way].at[1, :, cols(p)]
        else:
            s, d = zz[way].at[1, :, cols(p)], zz[way].at[2, :, cols(p)]
        return remote(s, d, s_z.at[p, way, kind], r_z.at[p, way, kind], z_sides[way])

    def z_first(p):
        for way in range(2):
            @pl.when(target(way, 4)[1])
            def _(way=way):
                copy_z(p, way, 0).start()

            @pl.when(target(way, 3)[1])
            def _(way=way):
                copy_z(p, way, 2).start()

    def z_step(p, k):
        for way in range(2):
            @pl.when(target(way, k)[1])
            def _(way=way):
                b, _ = target(way, k)
                if k == 3:
                    copy_z(p, way, 0).wait_recv()
                    z4[way][:, cols(p)] = z4[way][:, cols(p)] + part[b, x, trav[way], cols(p)]
                    copy_z(p, way, 1).start()
                else:
                    got = 2 - k
                    if k == 2:
                        copy_z(p, way, 1).wait_recv()
                        copy_z(p, way, 2).wait_recv()
                    else:
                        copy_z(p, way, 3).wait_recv()
                    zz[way][got, :, cols(p)] = zz[way][got, :, cols(p)] + part[b, x, :, cols(p)]
                    copy_z(p, way, 5 - k).start()

    def copy_c(p):
        return remote(
            part.at[zl, x, pl.ds((1 - c) * 32, 32), cols(p)], fin.at[:, cols(p)], s_c.at[p], r_c.at[p], d_mate
        )

    def z_final(p):
        @pl.when(home)
        def _():
            copy_z(p, 0, 4).wait_recv()
            copy_z(p, 1, 4).wait_recv()
            part[zl, x, :, cols(p)] = part[zl, x, :, cols(p)] + (zp[2, :, cols(p)] + zm[2, :, cols(p)])
            copy_c(p).start()
            fin[:, cols(p)] = part[zl, x, pl.ds(c * 32, 32), cols(p)]

    olds = (old_a, old_g)
    block = zl * 2 + lax.div(x, 2)

    def make_shard(p):
        @pl.when(jnp.logical_not(home))
        def _():
            copy_c(p).wait_recv()
        total = jnp.maximum(fin[0:1, 640:641], F32(1.0))
        at = ALL_COLS[p]
        if p < 2:
            ext[:, 0:FEAT] = olds[p][0]
            ext[:, FEAT:EXT] = olds[p][0, :, 0:EXT - FEAT]
            old = ext[:, pl.ds(pl.multiple_of(block * 128, 128), WIN)]
            begin = SUM_COLS[p][0]
            full[zl, x, c, :, at[0]:at[0] + WIN] = 0.5 * old + 0.5 * (fin[:, begin:begin + WIN] / total)
        else:
            begin = SUM_COLS[p][0]
            full[zl, x, c, :, at[0]:at[0] + FEAT] = fin[:, begin:begin + FEAT] / total

    def acols(p):
        return pl.ds(ALL_COLS[p][0], ALL_COLS[p][1])

    def copy_gz(p, way, step):
        origin = zl - (step - 1) if way == 0 else zl + (step - 1)
        ok = jnp.logical_and(origin >= 0, zl < 3) if way == 0 else jnp.logical_and(origin <= 3, zl > 0)
        ref = full.at[jnp.clip(origin, 0, 3), x, c, :, acols(p)]
        return ok, remote(ref, ref, s_gz.at[p, way, step - 1], r_gz.at[p, way, step - 1], z_sides[way])

    def gz_send(p, step):
        for way in range(2):
            ok, cp = copy_gz(p, way, step)
            @pl.when(ok)
            def _(cp=cp):
                cp.start()

    def gz_wait(p, step):
        for way in range(2):
            ok = zl - step >= 0 if way == 0 else zl + step <= 3
            cp = copy_gz(p, way, step)[1]
            @pl.when(ok)
            def _(cp=cp):
                cp.wait_recv()

    def copy_gx(p, way, kind):
        if kind == 0:
            ref = full.at[:, x, c, :, acols(p)]
        else:
            who = left if way == 0 else right
            ref = full.at[:, who, c, pl.ds(16 * way, 16), acols(p)]
        return remote(ref, ref, s_gx.at[p, way, kind], r_gx.at[p, way, kind], sides[way])

    def copy_gc(p, i):
        who = (x, left, right, opp)[i]
        ref = full.at[:, who, c, :, acols(p)]
        return remote(ref, ref, s_gc.at[p, i], r_gc.at[p, i], d_mate)

    def gx_send(p):
        for way in range(2):
            copy_gx(p, way, 0).start()
        copy_gc(p, 0).start()

    def gx_forward(p):
        for way in range(2):
            copy_gx(p, way, 0).wait_recv()
            copy_gx(p, way, 1).start()
            copy_gc(p, 1 + way).start()

    def gx_last(p):
        for way in range(2):
            copy_gx(p, way, 1).wait_recv()
        copy_gc(p, 3).start()

    def g_wait(p):
        for i in range(4):
            copy_gc(p, i).wait_recv()

    for cp in locals_:
        cp.wait()
    first_rows(0)
    send_rows(1)
    second_rows(0)
    last_rows(0)
    for cp in quick:
        cp.wait_recv()
    held = jnp.zeros((8, ROWS), F32)
    for s in range(8):
        row = posb[s, pl.ds(lane, 1), :]
        held = held + jnp.where(row >= 0, F32(1.0), F32(0.0))
    count = jnp.sum(held[0:1, :])
    part[:, :, :, 640:768] = jnp.full((4, 4, 64, 128), count, F32)
    mate_rows(0)
    pack(0)
    factor_gram(0, 0, 2)
    first_rows(1)
    factor_gram(0, 2, 4)
    x_send(0, 0)
    x_send(0, 1)
    second_rows(1)
    x_relay(0)
    last_rows(1)
    mate_rows(1)
    pack(1)
    factor_gram(1, 0, 4)
    x_send(1, 0)
    x_send(1, 1)
    x_final(0)
    z_first(0)
    cross_gram(0, 2)
    z_step(0, 3)
    cross_gram(2, 4)
    z_step(0, 2)
    x_relay(1)
    x_send(2, 0)
    x_send(2, 1)
    z_step(0, 1)
    z_final(0)
    x_final(1)
    z_first(1)
    make_shard(0)
    gz_send(0, 1)
    z_step(1, 3)
    gz_wait(0, 1)
    gz_send(0, 2)
    z_step(1, 2)
    gz_wait(0, 2)
    gz_send(0, 3)
    x_relay(2)
    z_step(1, 1)
    z_final(1)
    make_shard(1)
    gz_send(1, 1)
    gz_wait(0, 3)
    gx_send(0)
    gz_wait(1, 1)
    gz_send(1, 2)
    gz_wait(1, 2)
    gz_send(1, 3)
    gz_wait(1, 3)
    gx_send(1)
    x_final(2)
    z_first(2)
    gx_forward(0)
    z_step(2, 3)
    z_step(2, 2)
    gx_forward(1)
    z_step(2, 1)
    z_final(2)
    make_shard(2)
    gz_send(2, 1)
    gx_last(0)
    gz_wait(2, 1)
    gz_send(2, 2)
    gx_last(1)
    gz_wait(2, 2)
    gz_send(2, 3)
    for cp in started:
        cp.wait_send()
    gz_wait(2, 3)
    gx_send(2)

    fac = raw_a
    row_ids = lax.broadcasted_iota(jnp.int32, (128, FEAT), 0)
    col_ids = lax.broadcasted_iota(jnp.int32, (128, FEAT), 1)
    alphas, damps = [], []
    for t in range(2):
        g_wait(t)
        first = ALL_COLS[t][0]

        def rows_of(i, first_col):
            b, h = lax.div(i, 2), lax.rem(i, 2)
            got = full[b, pl.ds(h * 2, 2), :, :, first_col]
            return got.reshape(128, 128)

        def build(i, tr, t=t, first=first):
            for k in range(8):
                j = lax.rem(i + k, 8)
                if k <= 4:
                    blk = rows_of(i, pl.ds(first + k * 128, 128))
                else:
                    blk = rows_of(j, pl.ds(first + (8 - k) * 128, 128)).T
                if k == 0:
                    tr = tr + jnp.sum(jnp.where(row_ids[:, :128] == col_ids[:, :128], blk, F32(0.0)))
                fac[pl.ds(pl.multiple_of(t * FEAT + i * 128, 128), 128), pl.ds(pl.multiple_of(j * 128, 128), 128)] = blk
            return tr

        trace = lax.fori_loop(0, 8, build, F32(0.0))
        damp = F32(0.1) * trace / F32(FEAT)

        def shift(i, best, t=t, damp=damp, row=0, col=t * FEAT, skip=0):
            at = pl.ds(pl.multiple_of(row + (i - skip) * 128, 128), 128)
            m = fac[pl.ds(pl.multiple_of(t * FEAT + i * 128, 128), 128), :] + jnp.where(
                row_ids + i * 128 == col_ids, damp, F32(0.0))
            hi, lo = split(m)
            pkh[at, col:col + FEAT] = hi
            pkl[at, col:col + FEAT] = lo
            return jnp.maximum(best, jnp.max(jnp.sum(jnp.abs(m), axis=1, keepdims=True)))

        best = lax.fori_loop(0, 6, shift, F32(0.0))
        best = lax.fori_loop(
            6, 8, lambda i, best, t=t: shift(i, best, row=t * 256, col=2 * FEAT, skip=6), best)
        alphas.append(F32(1.0) / jnp.full((1, 1), best, F32))
        damps.append(damp)
        if t == 0:
            gx_forward(2)
        else:
            gx_last(2)

    d = zl * 8 + x * 2 + c
    mine = pl.ds(pl.multiple_of(d * 32, 32), 32)
    mine_g = pl.ds(pl.multiple_of(FEAT + d * 32, 32), 32)
    out[0] = fac[mine, :]
    out[1] = fac[mine_g, :]

    def times(v, t):
        hi, lo = split(v)
        both = jnp.concatenate([hi, lo], axis=0)
        parts = []
        for nb in range(4):
            at = slice(t * FEAT + nb * 256, t * FEAT + nb * 256 + 256)
            low = slice(2 * FEAT + nb * 256, 2 * FEAT + nb * 256 + 256)
            end = slice(t * 256, t * 256 + 256)
            one = dot(both[:, :SLOTS], pkh[:, at]) + dot(both[:, SLOTS:], pkh[end, low])
            fine = dot(hi[:, :SLOTS], pkl[:, at]) + dot(hi[:, SLOTS:], pkl[end, low])
            parts.append(one[:32] + (one[32:] + fine))
        return jnp.concatenate(parts, axis=1)

    aa, ag = alphas
    unit_rows = jnp.where(
        lax.broadcasted_iota(jnp.int32, (32, FEAT), 0) + d * 32
        == lax.broadcasted_iota(jnp.int32, (32, FEAT), 1), F32(1.0), F32(0.0))
    shifted_rows = fac[mine_g, :] + damps[1] * unit_rows
    u1 = ag * (2.0 * unit_rows - ag * shifted_rows)
    u2 = times(u1, 1)
    inv_rows = 2.0 * u1 - ag * (2.0 * u2 - ag * times(u2, 1))
    g_wait(2)
    hi, lo = split(inv_rows)
    both = jnp.concatenate([hi, lo], axis=0)
    parts = []
    for nb in range(4):
        rh, rl = split(full[:, :, :, :, 1280 + nb * 256:1536 + nb * 256].reshape(FEAT, 256))
        one = dot(both, rh)
        parts.append(one[:32] + (one[32:] + dot(hi, rl)))
    lhs = jnp.concatenate(parts, axis=1)
    half_way = aa * (2.0 * lhs - aa * times(lhs, 0))
    w = times(half_way, 0)
    out[2] = 2.0 * half_way - aa * (2.0 * w - aa * times(w, 0))

    for p in range(3):
        for way in range(2):
            for kind in range(3):
                copy_x(p, way, kind).wait_send()
            for kind in range(5):
                k = (4, 3, 3, 2, 1)[kind]
                @pl.when(target(way, k)[1])
                def _(p=p, way=way, kind=kind):
                    copy_z(p, way, kind).wait_send()
            for step in range(1, 4):
                ok, cp = copy_gz(p, way, step)
                @pl.when(ok)
                def _(cp=cp):
                    cp.wait_send()
            for kind in range(2):
                copy_gx(p, way, kind).wait_send()
        @pl.when(home)
        def _(p=p):
            copy_c(p).wait_send()
        for i in range(4):
            copy_gc(p, i).wait_send()


def finish_kernel(got, mom, wts, out_a, out_g, out_m, out_w):
    out_a[0] = got[0]
    out_g[0] = got[1]
    moment = 0.9 * mom[0] + got[2]
    out_m[0] = moment
    out_w[0] = wts[0] - 0.5 * moment


def on_device(acts, grads_out, routes, counts, old_act_factor, old_grad_factor, momentum, weights):
    experts = jnp.arange(8, dtype=jnp.int32)
    hit = jnp.sum(
        (routes.T[:, None, :] == experts[None, :, None]).astype(jnp.int32), axis=0, dtype=jnp.int32
    )
    rank = jnp.cumsum(hit, axis=1, dtype=jnp.int32) - hit
    kept = (hit > 0) & (rank < counts[0][:, None])
    pos = jnp.where(kept, rank, -1)
    vm = pl.BlockSpec(memory_space=pltpu.VMEM)
    hbm = pl.BlockSpec(memory_space=pl.ANY)
    dma = pltpu.SemaphoreType.DMA
    got = pl.pallas_call(
        step_kernel,
        out_shape=jax.ShapeDtypeStruct((3, 32, FEAT), F32),
        in_specs=[hbm, hbm, hbm, vm, vm],
        out_specs=vm,
        scratch_shapes=[
            pltpu.VMEM((8 * ROWS, FEAT), F32),
            pltpu.VMEM((8 * ROWS, FEAT), F32),
            pltpu.VMEM((8, 8, ROWS), jnp.int32),
            pltpu.VMEM((SLOTS, 2 * EXT), BF16),
            pltpu.VMEM((SLOTS, 2 * EXT), BF16),
            pltpu.VMEM((4, 4, 64, SUM_W), F32),
            pltpu.VMEM((2, 4, 32, SUM_W), F32),
            pltpu.VMEM((2, 4, 32, SUM_W), F32),
            pltpu.VMEM((2, 4, 32, SUM_W), F32),
            pltpu.VMEM((32, SUM_W), F32),
            pltpu.VMEM((32, SUM_W), F32),
            pltpu.VMEM((3, 64, SUM_W), F32),
            pltpu.VMEM((3, 64, SUM_W), F32),
            pltpu.VMEM((32, SUM_W), F32),
            pltpu.VMEM((4, 4, 2, 32, ALL_W), F32),
            pltpu.VMEM((32, EXT), F32),
            dma((3,)), dma((2, 2, 2)), dma((2, 2, 2)), dma((2, 2)), dma((2, 2)),
            dma((4, 2, 2)), dma((4, 2, 2)), dma((8,)), dma((8,)),
            dma((3, 2, 3)), dma((3, 2, 3)), dma((3, 2, 5)), dma((3, 2, 5)), dma((3,)), dma((3,)),
            dma((3, 2, 3)), dma((3, 2, 3)), dma((3, 2, 2)), dma((3, 2, 2)), dma((3, 4)), dma((3, 4)),
        ],
        compiler_params=pltpu.CompilerParams(
            collective_id=0, has_side_effects=True, vmem_limit_bytes=67043328
        ),
        name="step",
    )(acts, grads_out, pos, old_act_factor, old_grad_factor)
    out = jax.ShapeDtypeStruct((1, 32, FEAT), F32)
    return pl.pallas_call(
        finish_kernel,
        out_shape=(out, out, out, out),
        in_specs=[vm] * 3,
        out_specs=[vm] * 4,
        name="finish",
    )(got, momentum, weights)


def solution(mesh):
    rows = P(("dp", "expert"), None)
    mats = P("expert", "dp", None)
    return jax.shard_map(
        on_device,
        mesh=mesh,
        in_specs=(rows, rows, rows, rows, mats, mats, mats, mats),
        out_specs=(mats, mats, mats, mats),
        check_vma=False,
    )
```

```python
import jax
import jax.numpy as jnp
from jax import lax
from jax.experimental import pallas as pl
from jax.experimental.pallas import tpu as pltpu
from jax.sharding import PartitionSpec as P

MESH = pl.DeviceIdType.MESH
F32 = jnp.float32
BF16 = jnp.bfloat16
ROWS = 256
FEAT = 1024
CAP = 96
SLOTS = 8 * CAP
WIN = 640
EXT = 1536
SUM_COLS = ((0, 640), (640, 640), (1280, 1024))
SUM_W = 2304
ALL_COLS = ((0, 640), (640, 640), (1280, 1024))
ALL_W = 2304


def coords():
    dp = lax.axis_index("dp")
    ex = lax.axis_index("expert")
    c = lax.rem(dp, 2)
    x = lax.rem(lax.div(dp, 2), 4)
    zl = lax.div(dp, 8)
    y = lax.rem(ex, 4)
    zh = lax.div(ex, 4)
    return x, y, zl, zh, c


def device(x, y, z, c):
    return (lax.rem(z, 4) * 8 + x * 2 + c, lax.div(z, 4) * 4 + y)


def remote(src, dst, send, recv, dev):
    return pltpu.make_async_remote_copy(
        src_ref=src, dst_ref=dst, send_sem=send, recv_sem=recv, device_id=dev, device_id_type=MESH
    )


def dot(a, b):
    return jnp.dot(a, b, preferred_element_type=F32)


def dot_t(a, b):
    return lax.dot_general(a, b, (((0,), (0,)), ((), ())), preferred_element_type=F32)


def split(v):
    hi = v.astype(BF16)
    return hi, (v - hi.astype(F32)).astype(BF16)


def step_kernel(
    acts, grads, routes, counts, old_a, old_g, out,
    raw_a, raw_g, posb, pkh, pkl, part,
    x1, x2a, x2b, z4p, z4m, zp, zm, fin, full, ext,
    loc, s_y, r_y, s_f, r_f, s_p, r_p, s_q, r_q,
    s_x, r_x, s_z, r_z, s_c, r_c, s_gz, r_gz, s_gx, r_gx, s_gc, r_gc,
):
    x, y, zl, zh, c = coords()
    z = zh * 4 + zl
    right, left, opp = lax.rem(x + 1, 4), lax.rem(x + 3, 4), lax.rem(x + 2, 4)
    d_right, d_left = device(right, y, z, c), device(left, y, z, c)
    d_ztop, d_zlow = device(x, y, lax.rem(z + 1, 8), c), device(x, y, lax.rem(z + 7, 8), c)
    up, down, far = lax.rem(y + 1, 4), lax.rem(y + 3, 4), lax.rem(y + 2, 4)
    d_up, d_down, d_mate = device(x, up, z, c), device(x, down, z, c), device(x, y, z, 1 - c)
    peers = [
        d_up, d_down, device(x, far, z, c), d_mate,
        device(x, up, z, 1 - c), device(x, down, z, 1 - c), device(x, far, z, 1 - c),
    ]
    barrier = pltpu.get_barrier_semaphore()
    for peer in peers + [d_right, d_left, d_ztop, d_zlow]:
        pl.semaphore_signal(barrier, inc=1, device_id=peer, device_id_type=MESH)
    pl.semaphore_wait(barrier, 11)

    src = (acts, grads)
    raw = (raw_a, raw_g)

    def piece(t, slot, half):
        return raw[t].at[pl.ds(slot * ROWS + half * 128, 128), :]

    def own(t, half):
        return src[t].at[pl.ds(half * 128, 128), :]

    started = []

    def go(cp):
        cp.start()
        started.append(cp)

    locals_ = [
        pltpu.make_async_copy(src[t], raw[t].at[pl.ds(0, ROWS), :], loc.at[t]) for t in range(2)
    ]
    for cp in locals_:
        cp.start()
    toward = (d_up, d_down)
    direct, forward, mate = {}, {}, {}

    def send_rows(t):
        for turn in range(2):
            for way in range(2):
                half = turn ^ way
                direct[way, t, half] = remote(
                    own(t, half), piece(t, 1 + way, half), s_y.at[way, t, half],
                    r_y.at[way, t, half], toward[way],
                )
                go(direct[way, t, half])
        for half in range(2):
            mate[0, t, half] = remote(
                own(t, half), piece(t, 4, half), s_p.at[0, t, half], r_p.at[0, t, half], d_mate
            )
            go(mate[0, t, half])

    send_rows(0)
    expert_ids = lax.broadcasted_iota(jnp.int32, (8, ROWS), 0)
    hit = jnp.where(routes[0:1, :] == expert_ids, F32(1.0), F32(0.0)) + jnp.where(
        routes[1:2, :] == expert_ids, F32(1.0), F32(0.0))
    before = jnp.where(
        lax.broadcasted_iota(jnp.int32, (ROWS, ROWS), 0) < lax.broadcasted_iota(jnp.int32, (ROWS, ROWS), 1),
        F32(1.0), F32(0.0)).astype(BF16)
    rank = dot(hit.astype(BF16), before)
    square = lax.broadcasted_iota(jnp.int32, (8, 8), 0) == lax.broadcasted_iota(jnp.int32, (8, 8), 1)
    limit = jnp.sum(
        jnp.where(square, jnp.broadcast_to(counts[...].astype(F32), (8, 8)), F32(0.0)), axis=1, keepdims=True)
    posb[0] = jnp.where(jnp.logical_and(hit > 0.0, rank < limit), rank, F32(-1.0))
    quick = []
    for i, peer in enumerate(peers):
        quick.append(remote(posb.at[0], posb.at[i + 1], s_q.at[i + 1], r_q.at[i + 1], peer))
        go(quick[-1])

    def relay(slot, t, half):
        mate[slot, t, half] = remote(
            piece(t, slot, half), piece(t, 4 + slot, half), s_p.at[slot, t, half],
            r_p.at[slot, t, half], d_mate,
        )
        go(mate[slot, t, half])

    lane = c * 4 + y
    slot_ids = lax.broadcasted_iota(jnp.int32, (CAP, ROWS), 0).astype(F32)

    def pack(t):
        def body(s, carry):
            row = posb[s, pl.ds(lane, 1), :]
            sel = jnp.where(slot_ids == row, F32(1.0), F32(0.0)).astype(BF16)
            at = pl.ds(pl.multiple_of(s * CAP, CAP), CAP)
            for cb in range(4):
                v = raw[t][pl.ds(pl.multiple_of(s * ROWS, ROWS), ROWS), cb * 256:(cb + 1) * 256]
                hi, lo = split(v)
                for part, dest in ((hi, pkh), (lo, pkl)):
                    got = dot(sel, part).astype(BF16)
                    base = t * EXT + cb * 256
                    dest[at, base:base + 256] = got
                    if cb < 2:
                        dest[at, base + FEAT:base + FEAT + 256] = got
            return carry

        lax.fori_loop(0, 8, body, 0)

    def gram(lhs, rhs, width, store, begin_block, end_block):
        def body(ib, carry):
            at = pl.multiple_of(ib * 256, 256)
            lh = pkh[:, pl.ds(lhs + at, 256)]
            ll = pkl[:, pl.ds(lhs + at, 256)]
            for nb in range(width // 256):
                begin = rhs(at) + nb * 256
                rh = pkh[:, pl.ds(begin, 256)]
                rl = pkl[:, pl.ds(begin, 256)]
                store(ib, nb, dot_t(lh, rh) + (dot_t(lh, rl) + dot_t(ll, rh)))
            return carry

        lax.fori_loop(begin_block, end_block, body, 0)

    def window_store(first):
        def store(ib, nb, got):
            lo, hi = nb * 256, nb * 256 + 256
            keep = min(hi, WIN)
            part[ib, 0:2, :, first + lo:first + keep] = got[:128, :keep - lo].reshape(2, 64, keep - lo)
            begin = max(lo - 128, 0)
            part[ib, 2:4, :, first + begin:first + hi - 128] = got[128:, begin + 128 - lo:].reshape(
                2, 64, hi - 128 - begin)
        return store

    def cross_store(ib, nb, got):
        part[ib, :, :, 1280 + nb * 256:1280 + nb * 256 + 256] = got.reshape(4, 64, 256)

    def factor_gram(t, begin_block, end_block):
        gram(t * EXT, lambda at: t * EXT + at, 768, window_store(SUM_COLS[t][0]), begin_block, end_block)

    def cross_gram(begin_block, end_block):
        gram(EXT, lambda at: 0, FEAT, cross_store, begin_block, end_block)

    def first_rows(t):
        for way in range(2):
            direct[way, t, way].wait_recv()
            forward[way, t] = remote(
                piece(t, 1 + way, way), piece(t, 3, way), s_f.at[way, t], r_f.at[way, t], toward[way]
            )
            go(forward[way, t])
            relay(1 + way, t, way)

    def second_rows(t):
        for way in range(2):
            direct[way, t, 1 - way].wait_recv()
            relay(1 + way, t, 1 - way)

    def last_rows(t):
        for way in range(2):
            forward[way, t].wait_recv()
            relay(3, t, way)

    def mate_rows(t):
        for slot in range(4):
            for half in range(2):
                mate[slot, t, half].wait_recv()

    home = zh == c
    sides = (d_right, d_left)
    near = (right, left)
    lo_half, hi_half = pl.ds(0, 32), pl.ds(32, 32)
    trav, rest = (lo_half, hi_half), (hi_half, lo_half)

    def cols(p):
        return pl.ds(SUM_COLS[p][0], SUM_COLS[p][1])

    def copy_x(p, way, kind):
        if kind == 0:
            s, d = part.at[:, opp, trav[way], cols(p)], x1.at[way, :, :, cols(p)]
        elif kind == 1:
            s, d = part.at[:, near[way], rest[way], cols(p)], x2b.at[way, :, :, cols(p)]
        else:
            s, d = x1.at[way, :, :, cols(p)], x2a.at[way, :, :, cols(p)]
        return remote(s, d, s_x.at[p, way, kind], r_x.at[p, way, kind], sides[way])

    def x_send(p, kind):
        for way in range(2):
            copy_x(p, way, kind).start()

    def x_relay(p):
        for way in range(2):
            copy_x(p, way, 0).wait_recv()

            def body(b, carry):
                x1[way, b, :, cols(p)] = x1[way, b, :, cols(p)] + part[b, near[way], trav[way], cols(p)]
                return carry

            lax.fori_loop(0, 4, body, 0)
        x_send(p, 2)

    def x_final(p):
        for way in range(2):
            copy_x(p, way, 1).wait_recv()
            copy_x(p, way, 2).wait_recv()

        def body(b, carry):
            part[b, x, lo_half, cols(p)] = part[b, x, lo_half, cols(p)] + (
                x2a[0, b, :, cols(p)] + x2b[1, b, :, cols(p)])
            part[b, x, hi_half, cols(p)] = part[b, x, hi_half, cols(p)] + (
                x2a[1, b, :, cols(p)] + x2b[0, b, :, cols(p)])
            return carry

        lax.fori_loop(0, 4, body, 0)

    z_sides = (d_ztop, d_zlow)
    z4 = (z4p, z4m)
    zz = (zp, zm)

    def target(way, k):
        zd = lax.rem(z + k, 8) if way == 0 else lax.rem(z + 8 - k, 8)
        return lax.rem(zd, 4), lax.div(zd, 4) == c

    def copy_z(p, way, kind):
        k = (4, 3, 3, 2, 1)[kind]
        b, _ = target(way, k)
        if kind == 0:
            s, d = part.at[b, x, trav[way], cols(p)], z4[way].at[:, cols(p)]
        elif kind == 1:
            s, d = z4[way].at[:, cols(p)], zz[way].at[0, trav[way], cols(p)]
        elif kind == 2:
            s, d = part.at[b, x, rest[way], cols(p)], zz[way].at[0, rest[way], cols(p)]
        elif kind == 3:
            s, d = zz[way].at[0, :, cols(p)], zz[way].at[1, :, cols(p)]
        else:
            s, d = zz[way].at[1, :, cols(p)], zz[way].at[2, :, cols(p)]
        return remote(s, d, s_z.at[p, way, kind], r_z.at[p, way, kind], z_sides[way])

    def z_first(p):
        for way in range(2):
            @pl.when(target(way, 4)[1])
            def _(way=way):
                copy_z(p, way, 0).start()

            @pl.when(target(way, 3)[1])
            def _(way=way):
                copy_z(p, way, 2).start()

    def z_step(p, k):
        for way in range(2):
            @pl.when(target(way, k)[1])
            def _(way=way):
                b, _ = target(way, k)
                if k == 3:
                    copy_z(p, way, 0).wait_recv()
                    z4[way][:, cols(p)] = z4[way][:, cols(p)] + part[b, x, trav[way], cols(p)]
                    copy_z(p, way, 1).start()
                else:
                    got = 2 - k
                    if k == 2:
                        copy_z(p, way, 1).wait_recv()
                        copy_z(p, way, 2).wait_recv()
                    else:
                        copy_z(p, way, 3).wait_recv()
                    zz[way][got, :, cols(p)] = zz[way][got, :, cols(p)] + part[b, x, :, cols(p)]
                    copy_z(p, way, 5 - k).start()

    def copy_c(p):
        return remote(
            part.at[zl, x, pl.ds((1 - c) * 32, 32), cols(p)], fin.at[:, cols(p)], s_c.at[p], r_c.at[p], d_mate
        )

    def z_final(p):
        @pl.when(home)
        def _():
            copy_z(p, 0, 4).wait_recv()
            copy_z(p, 1, 4).wait_recv()
            part[zl, x, :, cols(p)] = part[zl, x, :, cols(p)] + (zp[2, :, cols(p)] + zm[2, :, cols(p)])
            copy_c(p).start()
            fin[:, cols(p)] = part[zl, x, pl.ds(c * 32, 32), cols(p)]

    olds = (old_a, old_g)
    block = zl * 2 + lax.div(x, 2)

    def make_shard(p):
        @pl.when(jnp.logical_not(home))
        def _():
            copy_c(p).wait_recv()
        total = jnp.maximum(fin[8:9, 512:513], F32(1.0))
        at = ALL_COLS[p]
        if p < 2:
            ext[:, 0:FEAT] = olds[p][0]
            ext[:, FEAT:EXT] = olds[p][0, :, 0:EXT - FEAT]
            old = ext[:, pl.ds(pl.multiple_of(block * 128, 128), WIN)]
            begin = SUM_COLS[p][0]
            full[zl, x, c, :, at[0]:at[0] + WIN] = 0.5 * old + 0.5 * (fin[:, begin:begin + WIN] / total)
        else:
            begin = SUM_COLS[p][0]
            full[zl, x, c, :, at[0]:at[0] + FEAT] = fin[:, begin:begin + FEAT] / total

    def acols(p):
        return pl.ds(ALL_COLS[p][0], ALL_COLS[p][1])

    def copy_gz(p, way, step):
        origin = zl - (step - 1) if way == 0 else zl + (step - 1)
        ok = jnp.logical_and(origin >= 0, zl < 3) if way == 0 else jnp.logical_and(origin <= 3, zl > 0)
        ref = full.at[jnp.clip(origin, 0, 3), x, c, :, acols(p)]
        return ok, remote(ref, ref, s_gz.at[p, way, step - 1], r_gz.at[p, way, step - 1], z_sides[way])

    def gz_send(p, step):
        for way in range(2):
            ok, cp = copy_gz(p, way, step)
            @pl.when(ok)
            def _(cp=cp):
                cp.start()

    def gz_wait(p, step):
        for way in range(2):
            ok = zl - step >= 0 if way == 0 else zl + step <= 3
            cp = copy_gz(p, way, step)[1]
            @pl.when(ok)
            def _(cp=cp):
                cp.wait_recv()

    def copy_gx(p, way, kind):
        if kind == 0:
            ref = full.at[:, x, c, :, acols(p)]
        else:
            who = left if way == 0 else right
            ref = full.at[:, who, c, pl.ds(16 * way, 16), acols(p)]
        return remote(ref, ref, s_gx.at[p, way, kind], r_gx.at[p, way, kind], sides[way])

    def copy_gc(p, i):
        who = (x, left, right, opp)[i]
        ref = full.at[:, who, c, :, acols(p)]
        return remote(ref, ref, s_gc.at[p, i], r_gc.at[p, i], d_mate)

    def gx_send(p):
        for way in range(2):
            copy_gx(p, way, 0).start()
        copy_gc(p, 0).start()

    def gx_forward(p):
        for way in range(2):
            copy_gx(p, way, 0).wait_recv()
            copy_gx(p, way, 1).start()
            copy_gc(p, 1 + way).start()

    def gx_last(p):
        for way in range(2):
            copy_gx(p, way, 1).wait_recv()
        copy_gc(p, 3).start()

    def g_wait(p):
        for i in range(4):
            copy_gc(p, i).wait_recv()

    for cp in locals_:
        cp.wait()
    first_rows(0)
    send_rows(1)
    second_rows(0)
    last_rows(0)
    for cp in quick:
        cp.wait_recv()
    held = jnp.zeros((8, ROWS), F32)
    for s in range(8):
        row = posb[s, pl.ds(lane, 1), :]
        held = held + jnp.where(row >= 0, F32(1.0), F32(0.0))
    count = jnp.sum(held[0:1, :])
    mate_rows(0)
    pack(0)
    factor_gram(0, 0, 2)
    first_rows(1)
    factor_gram(0, 2, 4)
    lanes = lax.broadcasted_iota(jnp.int32, (64, 128), 1)
    tops = lax.broadcasted_iota(jnp.int32, (64, 128), 0)
    for b in range(4):
        for xb in range(4):
            put = lanes == 0
            if b >= 2 and xb % 2 == 0:
                put = jnp.logical_and(put, tops > 0)
            part[b, xb, :, 512:640] = jnp.where(put, count, part[b, xb, :, 512:640])
    x_send(0, 0)
    x_send(0, 1)
    second_rows(1)
    x_relay(0)
    last_rows(1)
    mate_rows(1)
    pack(1)
    factor_gram(1, 0, 4)
    x_send(1, 0)
    x_send(1, 1)
    x_final(0)
    z_first(0)
    cross_gram(0, 2)
    z_step(0, 3)
    cross_gram(2, 4)
    z_step(0, 2)
    x_relay(1)
    x_send(2, 0)
    x_send(2, 1)
    z_step(0, 1)
    z_final(0)
    x_final(1)
    z_first(1)
    make_shard(0)
    gz_send(0, 1)
    z_step(1, 3)
    gz_wait(0, 1)
    gz_send(0, 2)
    z_step(1, 2)
    gz_wait(0, 2)
    gz_send(0, 3)
    x_relay(2)
    z_step(1, 1)
    z_final(1)
    make_shard(1)
    gz_send(1, 1)
    gz_wait(0, 3)
    gx_send(0)
    gz_wait(1, 1)
    gz_send(1, 2)
    gz_wait(1, 2)
    gz_send(1, 3)
    gz_wait(1, 3)
    gx_send(1)
    x_final(2)
    z_first(2)
    gx_forward(0)
    z_step(2, 3)
    z_step(2, 2)
    gx_forward(1)
    z_step(2, 1)
    z_final(2)
    make_shard(2)
    gz_send(2, 1)
    gx_last(0)
    gz_wait(2, 1)
    gz_send(2, 2)
    gx_last(1)
    gz_wait(2, 2)
    gz_send(2, 3)
    for cp in started:
        cp.wait_send()
    gz_wait(2, 3)
    gx_send(2)

    fac = raw_a
    row_ids = lax.broadcasted_iota(jnp.int32, (128, FEAT), 0)
    col_ids = lax.broadcasted_iota(jnp.int32, (128, FEAT), 1)
    alphas, damps = [], []
    for t in range(2):
        g_wait(t)
        first = ALL_COLS[t][0]

        def rows_of(i, first_col):
            b, h = lax.div(i, 2), lax.rem(i, 2)
            got = full[b, pl.ds(h * 2, 2), :, :, first_col]
            return got.reshape(128, 128)

        def build(i, tr, t=t, first=first):
            for k in range(8):
                j = lax.rem(i + k, 8)
                if k == 4 and t == 0:
                    i_low = lax.rem(i, 4)
                    one = rows_of(i_low, pl.ds(first + 512, 128))
                    two = rows_of(i_low + 4, pl.ds(first + 512, 128))
                    blk = jnp.where(
                        i < 4,
                        jnp.where(col_ids[:, :128] == 0, two.T, one),
                        jnp.where(row_ids[:, :128] == 0, two, one.T))
                elif k <= 4:
                    blk = rows_of(i, pl.ds(first + k * 128, 128))
                else:
                    blk = rows_of(j, pl.ds(first + (8 - k) * 128, 128)).T
                if k == 0:
                    tr = tr + jnp.sum(jnp.where(row_ids[:, :128] == col_ids[:, :128], blk, F32(0.0)))
                fac[pl.ds(pl.multiple_of(t * FEAT + i * 128, 128), 128), pl.ds(pl.multiple_of(j * 128, 128), 128)] = blk
            return tr

        trace = lax.fori_loop(0, 8, build, F32(0.0))
        damp = F32(0.1) * trace / F32(FEAT)

        def shift(i, best, t=t, damp=damp, row=0, col=t * FEAT, skip=0):
            at = pl.ds(pl.multiple_of(row + (i - skip) * 128, 128), 128)
            m = fac[pl.ds(pl.multiple_of(t * FEAT + i * 128, 128), 128), :] + jnp.where(
                row_ids + i * 128 == col_ids, damp, F32(0.0))
            hi, lo = split(m)
            pkh[at, col:col + FEAT] = hi
            pkl[at, col:col + FEAT] = lo
            return jnp.maximum(best, jnp.max(jnp.sum(jnp.abs(m), axis=1, keepdims=True)))

        best = lax.fori_loop(0, 6, shift, F32(0.0))
        best = lax.fori_loop(
            6, 8, lambda i, best, t=t: shift(i, best, row=t * 256, col=2 * FEAT, skip=6), best)
        alphas.append(F32(1.0) / jnp.full((1, 1), best, F32))
        damps.append(damp)
        if t == 0:
            gx_forward(2)
        else:
            gx_last(2)

    d = zl * 8 + x * 2 + c
    mine = pl.ds(pl.multiple_of(d * 32, 32), 32)
    mine_g = pl.ds(pl.multiple_of(FEAT + d * 32, 32), 32)
    out[0] = fac[mine, :]
    out[1] = fac[mine_g, :]

    def times(v, t):
        hi, lo = split(v)
        both = jnp.concatenate([hi, lo], axis=0)
        parts = []
        for nb in range(4):
            at = slice(t * FEAT + nb * 256, t * FEAT + nb * 256 + 256)
            low = slice(2 * FEAT + nb * 256, 2 * FEAT + nb * 256 + 256)
            end = slice(t * 256, t * 256 + 256)
            one = dot(both[:, :SLOTS], pkh[:, at]) + dot(both[:, SLOTS:], pkh[end, low])
            fine = dot(hi[:, :SLOTS], pkl[:, at]) + dot(hi[:, SLOTS:], pkl[end, low])
            parts.append(one[:32] + (one[32:] + fine))
        return jnp.concatenate(parts, axis=1)

    aa, ag = alphas
    unit_rows = jnp.where(
        lax.broadcasted_iota(jnp.int32, (32, FEAT), 0) + d * 32
        == lax.broadcasted_iota(jnp.int32, (32, FEAT), 1), F32(1.0), F32(0.0))
    shifted_rows = fac[mine_g, :] + damps[1] * unit_rows
    u1 = ag * (2.0 * unit_rows - ag * shifted_rows)
    u2 = times(u1, 1)
    inv_rows = 2.0 * u1 - ag * (2.0 * u2 - ag * times(u2, 1))
    g_wait(2)
    hi, lo = split(inv_rows)
    both = jnp.concatenate([hi, lo], axis=0)
    parts = []
    for nb in range(4):
        rh, rl = split(full[:, :, :, :, 1280 + nb * 256:1536 + nb * 256].reshape(FEAT, 256))
        one = dot(both, rh)
        parts.append(one[:32] + (one[32:] + dot(hi, rl)))
    lhs = jnp.concatenate(parts, axis=1)
    half_way = aa * (2.0 * lhs - aa * times(lhs, 0))
    w = times(half_way, 0)
    out[2] = 2.0 * half_way - aa * (2.0 * w - aa * times(w, 0))

    for p in range(3):
        for way in range(2):
            for kind in range(3):
                copy_x(p, way, kind).wait_send()
            for kind in range(5):
                k = (4, 3, 3, 2, 1)[kind]
                @pl.when(target(way, k)[1])
                def _(p=p, way=way, kind=kind):
                    copy_z(p, way, kind).wait_send()
            for step in range(1, 4):
                ok, cp = copy_gz(p, way, step)
                @pl.when(ok)
                def _(cp=cp):
                    cp.wait_send()
            for kind in range(2):
                copy_gx(p, way, kind).wait_send()
        @pl.when(home)
        def _(p=p):
            copy_c(p).wait_send()
        for i in range(4):
            copy_gc(p, i).wait_send()


def finish_kernel(got, mom, wts, out_a, out_g, out_m, out_w):
    out_a[0] = got[0]
    out_g[0] = got[1]
    moment = 0.9 * mom[0] + got[2]
    out_m[0] = moment
    out_w[0] = wts[0] - 0.5 * moment


def on_device(acts, grads_out, routes, counts, old_act_factor, old_grad_factor, momentum, weights):
    vm = pl.BlockSpec(memory_space=pltpu.VMEM)
    hbm = pl.BlockSpec(memory_space=pl.ANY)
    dma = pltpu.SemaphoreType.DMA
    got = pl.pallas_call(
        step_kernel,
        out_shape=jax.ShapeDtypeStruct((3, 32, FEAT), F32),
        in_specs=[hbm, hbm, vm, vm, vm, vm],
        out_specs=vm,
        scratch_shapes=[
            pltpu.VMEM((8 * ROWS, FEAT), F32),
            pltpu.VMEM((8 * ROWS, FEAT), F32),
            pltpu.VMEM((8, 8, ROWS), F32),
            pltpu.VMEM((SLOTS, 2 * EXT), BF16),
            pltpu.VMEM((SLOTS, 2 * EXT), BF16),
            pltpu.VMEM((4, 4, 64, SUM_W), F32),
            pltpu.VMEM((2, 4, 32, SUM_W), F32),
            pltpu.VMEM((2, 4, 32, SUM_W), F32),
            pltpu.VMEM((2, 4, 32, SUM_W), F32),
            pltpu.VMEM((32, SUM_W), F32),
            pltpu.VMEM((32, SUM_W), F32),
            pltpu.VMEM((3, 64, SUM_W), F32),
            pltpu.VMEM((3, 64, SUM_W), F32),
            pltpu.VMEM((32, SUM_W), F32),
            pltpu.VMEM((4, 4, 2, 32, ALL_W), F32),
            pltpu.VMEM((32, EXT), F32),
            dma((2,)), dma((2, 2, 2)), dma((2, 2, 2)), dma((2, 2)), dma((2, 2)),
            dma((4, 2, 2)), dma((4, 2, 2)), dma((8,)), dma((8,)),
            dma((3, 2, 3)), dma((3, 2, 3)), dma((3, 2, 5)), dma((3, 2, 5)), dma((3,)), dma((3,)),
            dma((3, 2, 3)), dma((3, 2, 3)), dma((3, 2, 2)), dma((3, 2, 2)), dma((3, 4)), dma((3, 4)),
        ],
        compiler_params=pltpu.CompilerParams(
            collective_id=0, has_side_effects=True, vmem_limit_bytes=67043328
        ),
        name="step",
    )(acts, grads_out, routes.T, counts, old_act_factor, old_grad_factor)
    out = jax.ShapeDtypeStruct((1, 32, FEAT), F32)
    return pl.pallas_call(
        finish_kernel,
        out_shape=(out, out, out, out),
        in_specs=[vm] * 3,
        out_specs=[vm] * 4,
        name="finish",
    )(got, momentum, weights)


def solution(mesh):
    rows = P(("dp", "expert"), None)
    mats = P("expert", "dp", None)
    return jax.shard_map(
        on_device,
        mesh=mesh,
        in_specs=(rows, rows, rows, rows, mats, mats, mats, mats),
        out_specs=(mats, mats, mats, mats),
        check_vma=False,
    )
```

```python
import jax
import jax.numpy as jnp
from jax import lax
from jax.experimental import pallas as pl
from jax.experimental.pallas import tpu as pltpu
from jax.sharding import PartitionSpec as P

MESH = pl.DeviceIdType.MESH
F32 = jnp.float32
BF16 = jnp.bfloat16
ROWS = 256
FEAT = 1024
CAP = 96
SLOTS = 8 * CAP
WIN = 640
EXT = 1536
SUM_COLS = ((0, 640), (640, 640), (1280, 1024))
SUM_W = 2304
ALL_COLS = ((0, 640), (640, 640), (1280, 1024))
ALL_W = 2304


def coords():
    dp = lax.axis_index("dp")
    ex = lax.axis_index("expert")
    c = lax.rem(dp, 2)
    x = lax.rem(lax.div(dp, 2), 4)
    zl = lax.div(dp, 8)
    y = lax.rem(ex, 4)
    zh = lax.div(ex, 4)
    return x, y, zl, zh, c


def device(x, y, z, c):
    return (lax.rem(z, 4) * 8 + x * 2 + c, lax.div(z, 4) * 4 + y)


def remote(src, dst, send, recv, dev):
    return pltpu.make_async_remote_copy(
        src_ref=src, dst_ref=dst, send_sem=send, recv_sem=recv, device_id=dev, device_id_type=MESH
    )


def dot(a, b):
    return jnp.dot(a, b, preferred_element_type=F32)


def dot_t(a, b):
    return lax.dot_general(a, b, (((0,), (0,)), ((), ())), preferred_element_type=F32)


def split(v):
    hi = v.astype(BF16)
    return hi, (v - hi.astype(F32)).astype(BF16)


def step_kernel(
    acts, grads, routes, counts, old_a, old_g, out,
    raw_a, raw_g, posb, pkh, pkl, part,
    x1, x2a, x2b, z4p, z4m, zp, zm, fin, full, ext,
    loc, s_y, r_y, s_f, r_f, s_p, r_p, s_q, r_q,
    s_x, r_x, s_z, r_z, s_c, r_c, s_gz, r_gz, s_gx, r_gx, s_gc, r_gc,
):
    x, y, zl, zh, c = coords()
    z = zh * 4 + zl
    right, left, opp = lax.rem(x + 1, 4), lax.rem(x + 3, 4), lax.rem(x + 2, 4)
    d_right, d_left = device(right, y, z, c), device(left, y, z, c)
    d_ztop, d_zlow = device(x, y, lax.rem(z + 1, 8), c), device(x, y, lax.rem(z + 7, 8), c)
    up, down, far = lax.rem(y + 1, 4), lax.rem(y + 3, 4), lax.rem(y + 2, 4)
    d_up, d_down, d_mate = device(x, up, z, c), device(x, down, z, c), device(x, y, z, 1 - c)
    peers = [
        d_up, d_down, device(x, far, z, c), d_mate,
        device(x, up, z, 1 - c), device(x, down, z, 1 - c), device(x, far, z, 1 - c),
    ]
    barrier = pltpu.get_barrier_semaphore()
    for peer in peers + [d_right, d_left, d_ztop, d_zlow]:
        pl.semaphore_signal(barrier, inc=1, device_id=peer, device_id_type=MESH)
    pl.semaphore_wait(barrier, 11)

    src = (acts, grads)
    raw = (raw_a, raw_g)

    def piece(t, slot, half):
        return raw[t].at[pl.ds(slot * ROWS + half * 128, 128), :]

    def own(t, half):
        return src[t].at[pl.ds(half * 128, 128), :]

    started = []

    def go(cp):
        cp.start()
        started.append(cp)

    locals_ = [
        pltpu.make_async_copy(src[t], raw[t].at[pl.ds(0, ROWS), :], loc.at[t]) for t in range(2)
    ]
    for cp in locals_:
        cp.start()
    toward = (d_up, d_down)
    direct, forward, mate = {}, {}, {}

    def send_rows(t):
        for turn in range(2):
            for way in range(2):
                half = turn ^ way
                direct[way, t, half] = remote(
                    own(t, half), piece(t, 1 + way, half), s_y.at[way, t, half],
                    r_y.at[way, t, half], toward[way],
                )
                go(direct[way, t, half])
        for half in range(2):
            mate[0, t, half] = remote(
                own(t, half), piece(t, 4, half), s_p.at[0, t, half], r_p.at[0, t, half], d_mate
            )
            go(mate[0, t, half])

    send_rows(0)
    expert_ids = lax.broadcasted_iota(jnp.int32, (8, ROWS), 0)
    hit = jnp.where(routes[0:1, :] == expert_ids, F32(1.0), F32(0.0)) + jnp.where(
        routes[1:2, :] == expert_ids, F32(1.0), F32(0.0))
    before = jnp.where(
        lax.broadcasted_iota(jnp.int32, (ROWS, ROWS), 0) < lax.broadcasted_iota(jnp.int32, (ROWS, ROWS), 1),
        F32(1.0), F32(0.0)).astype(BF16)
    rank = dot(hit.astype(BF16), before)
    square = lax.broadcasted_iota(jnp.int32, (8, 8), 0) == lax.broadcasted_iota(jnp.int32, (8, 8), 1)
    limit = jnp.sum(
        jnp.where(square, jnp.broadcast_to(counts[...].astype(F32), (8, 8)), F32(0.0)), axis=1, keepdims=True)
    posb[0] = jnp.where(jnp.logical_and(hit > 0.0, rank < limit), rank, F32(-1.0))
    quick = []
    for i, peer in enumerate(peers):
        quick.append(remote(posb.at[0], posb.at[i + 1], s_q.at[i + 1], r_q.at[i + 1], peer))
        go(quick[-1])

    def relay(slot, t, half):
        mate[slot, t, half] = remote(
            piece(t, slot, half), piece(t, 4 + slot, half), s_p.at[slot, t, half],
            r_p.at[slot, t, half], d_mate,
        )
        go(mate[slot, t, half])

    lane = c * 4 + y
    slot_ids = lax.broadcasted_iota(jnp.int32, (CAP, ROWS), 0).astype(F32)

    def pack(t):
        def body(s, carry):
            row = posb[s, pl.ds(lane, 1), :]
            sel = jnp.where(slot_ids == row, F32(1.0), F32(0.0)).astype(BF16)
            at = pl.ds(pl.multiple_of(s * CAP, CAP), CAP)
            for cb in range(4):
                v = raw[t][pl.ds(pl.multiple_of(s * ROWS, ROWS), ROWS), cb * 256:(cb + 1) * 256]
                hi, lo = split(v)
                for part, dest in ((hi, pkh), (lo, pkl)):
                    got = dot(sel, part).astype(BF16)
                    base = t * EXT + cb * 256
                    dest[at, base:base + 256] = got
                    if cb < 2:
                        dest[at, base + FEAT:base + FEAT + 256] = got
            return carry

        lax.fori_loop(0, 8, body, 0)

    def gram(lhs, rhs, width, store, begin_block, end_block):
        def body(ib, carry):
            at = pl.multiple_of(ib * 256, 256)
            lh = pkh[:, pl.ds(lhs + at, 256)]
            ll = pkl[:, pl.ds(lhs + at, 256)]
            for nb in range(width // 256):
                begin = rhs(at) + nb * 256
                rh = pkh[:, pl.ds(begin, 256)]
                rl = pkl[:, pl.ds(begin, 256)]
                store(ib, nb, dot_t(lh, rh) + (dot_t(lh, rl) + dot_t(ll, rh)))
            return carry

        lax.fori_loop(begin_block, end_block, body, 0)

    def window_store(first):
        def store(ib, nb, got):
            lo, hi = nb * 256, nb * 256 + 256
            keep = min(hi, WIN)
            part[ib, 0:2, :, first + lo:first + keep] = got[:128, :keep - lo].reshape(2, 64, keep - lo)
            begin = max(lo - 128, 0)
            part[ib, 2:4, :, first + begin:first + hi - 128] = got[128:, begin + 128 - lo:].reshape(
                2, 64, hi - 128 - begin)
        return store

    def cross_store(ib, nb, got):
        part[ib, :, :, 1280 + nb * 256:1280 + nb * 256 + 256] = got.reshape(4, 64, 256)

    def factor_gram(t, begin_block, end_block):
        gram(t * EXT, lambda at: t * EXT + at, 768, window_store(SUM_COLS[t][0]), begin_block, end_block)

    def cross_gram(begin_block, end_block):
        gram(EXT, lambda at: 0, FEAT, cross_store, begin_block, end_block)

    def first_rows(t):
        for way in range(2):
            direct[way, t, way].wait_recv()
            forward[way, t] = remote(
                piece(t, 1 + way, way), piece(t, 3, way), s_f.at[way, t], r_f.at[way, t], toward[way]
            )
            go(forward[way, t])
            relay(1 + way, t, way)

    def second_rows(t):
        for way in range(2):
            direct[way, t, 1 - way].wait_recv()
            relay(1 + way, t, 1 - way)

    def last_rows(t):
        for way in range(2):
            forward[way, t].wait_recv()
            relay(3, t, way)

    def mate_rows(t):
        for slot in range(4):
            for half in range(2):
                mate[slot, t, half].wait_recv()

    home = zh == c
    sides = (d_right, d_left)
    near = (right, left)
    lo_half, hi_half = pl.ds(0, 32), pl.ds(32, 32)
    trav, rest = (lo_half, hi_half), (hi_half, lo_half)

    def cols(p):
        return pl.ds(SUM_COLS[p][0], SUM_COLS[p][1])

    def copy_x(p, way, kind):
        if kind == 0:
            s, d = part.at[:, opp, trav[way], cols(p)], x1.at[way, :, :, cols(p)]
        elif kind == 1:
            s, d = part.at[:, near[way], rest[way], cols(p)], x2b.at[way, :, :, cols(p)]
        else:
            s, d = x1.at[way, :, :, cols(p)], x2a.at[way, :, :, cols(p)]
        return remote(s, d, s_x.at[p, way, kind], r_x.at[p, way, kind], sides[way])

    def x_send(p, kind):
        for way in range(2):
            copy_x(p, way, kind).start()

    def x_relay(p):
        for way in range(2):
            copy_x(p, way, 0).wait_recv()

            def body(b, carry):
                x1[way, b, :, cols(p)] = x1[way, b, :, cols(p)] + part[b, near[way], trav[way], cols(p)]
                return carry

            lax.fori_loop(0, 4, body, 0)
        x_send(p, 2)

    def x_final(p):
        for way in range(2):
            copy_x(p, way, 1).wait_recv()
            copy_x(p, way, 2).wait_recv()

        def body(b, carry):
            part[b, x, lo_half, cols(p)] = part[b, x, lo_half, cols(p)] + (
                x2a[0, b, :, cols(p)] + x2b[1, b, :, cols(p)])
            part[b, x, hi_half, cols(p)] = part[b, x, hi_half, cols(p)] + (
                x2a[1, b, :, cols(p)] + x2b[0, b, :, cols(p)])
            return carry

        lax.fori_loop(0, 4, body, 0)

    z_sides = (d_ztop, d_zlow)
    z4 = (z4p, z4m)
    zz = (zp, zm)

    def target(way, k):
        zd = lax.rem(z + k, 8) if way == 0 else lax.rem(z + 8 - k, 8)
        return lax.rem(zd, 4), lax.div(zd, 4) == c

    def copy_z(p, way, kind):
        k = (4, 3, 3, 2, 1)[kind]
        b, _ = target(way, k)
        if kind == 0:
            s, d = part.at[b, x, trav[way], cols(p)], z4[way].at[:, cols(p)]
        elif kind == 1:
            s, d = z4[way].at[:, cols(p)], zz[way].at[0, trav[way], cols(p)]
        elif kind == 2:
            s, d = part.at[b, x, rest[way], cols(p)], zz[way].at[0, rest[way], cols(p)]
        elif kind == 3:
            s, d = zz[way].at[0, :, cols(p)], zz[way].at[1, :, cols(p)]
        else:
            s, d = zz[way].at[1, :, cols(p)], zz[way].at[2, :, cols(p)]
        return remote(s, d, s_z.at[p, way, kind], r_z.at[p, way, kind], z_sides[way])

    def z_first(p):
        for way in range(2):
            @pl.when(target(way, 4)[1])
            def _(way=way):
                copy_z(p, way, 0).start()

            @pl.when(target(way, 3)[1])
            def _(way=way):
                copy_z(p, way, 2).start()

    def z_step(p, k):
        for way in range(2):
            @pl.when(target(way, k)[1])
            def _(way=way):
                b, _ = target(way, k)
                if k == 3:
                    copy_z(p, way, 0).wait_recv()
                    z4[way][:, cols(p)] = z4[way][:, cols(p)] + part[b, x, trav[way], cols(p)]
                    copy_z(p, way, 1).start()
                else:
                    got = 2 - k
                    if k == 2:
                        copy_z(p, way, 1).wait_recv()
                        copy_z(p, way, 2).wait_recv()
                    else:
                        copy_z(p, way, 3).wait_recv()
                    zz[way][got, :, cols(p)] = zz[way][got, :, cols(p)] + part[b, x, :, cols(p)]
                    copy_z(p, way, 5 - k).start()

    def copy_c(p):
        return remote(
            part.at[zl, x, pl.ds((1 - c) * 32, 32), cols(p)], fin.at[:, cols(p)], s_c.at[p], r_c.at[p], d_mate
        )

    def z_final(p):
        @pl.when(home)
        def _():
            copy_z(p, 0, 4).wait_recv()
            copy_z(p, 1, 4).wait_recv()
            part[zl, x, :, cols(p)] = part[zl, x, :, cols(p)] + (zp[2, :, cols(p)] + zm[2, :, cols(p)])
            copy_c(p).start()
            fin[:, cols(p)] = part[zl, x, pl.ds(c * 32, 32), cols(p)]

    olds = (old_a, old_g)
    block = zl * 2 + lax.div(x, 2)

    def make_shard(p):
        @pl.when(jnp.logical_not(home))
        def _():
            copy_c(p).wait_recv()
        total = jnp.maximum(fin[8:9, 512:513], F32(1.0))
        at = ALL_COLS[p]
        if p < 2:
            ext[:, 0:FEAT] = olds[p][0]
            ext[:, FEAT:EXT] = olds[p][0, :, 0:EXT - FEAT]
            old = ext[:, pl.ds(pl.multiple_of(block * 128, 128), WIN)]
            begin = SUM_COLS[p][0]
            full[zl, x, c, :, at[0]:at[0] + WIN] = 0.5 * old + 0.5 * (fin[:, begin:begin + WIN] / total)
        else:
            begin = SUM_COLS[p][0]
            full[zl, x, c, :, at[0]:at[0] + FEAT] = fin[:, begin:begin + FEAT] / total

    def acols(p):
        return pl.ds(ALL_COLS[p][0], ALL_COLS[p][1])

    def copy_gz(p, way, step):
        origin = zl - (step - 1) if way == 0 else zl + (step - 1)
        ok = jnp.logical_and(origin >= 0, zl < 3) if way == 0 else jnp.logical_and(origin <= 3, zl > 0)
        ref = full.at[jnp.clip(origin, 0, 3), x, c, :, acols(p)]
        return ok, remote(ref, ref, s_gz.at[p, way, step - 1], r_gz.at[p, way, step - 1], z_sides[way])

    def gz_send(p, step):
        for way in range(2):
            ok, cp = copy_gz(p, way, step)
            @pl.when(ok)
            def _(cp=cp):
                cp.start()

    def gz_wait(p, step):
        for way in range(2):
            ok = zl - step >= 0 if way == 0 else zl + step <= 3
            cp = copy_gz(p, way, step)[1]
            @pl.when(ok)
            def _(cp=cp):
                cp.wait_recv()

    def copy_gx(p, way, kind):
        if kind == 0:
            ref = full.at[:, x, c, :, acols(p)]
        else:
            who = left if way == 0 else right
            ref = full.at[:, who, c, pl.ds(16 * way, 16), acols(p)]
        return remote(ref, ref, s_gx.at[p, way, kind], r_gx.at[p, way, kind], sides[way])

    def copy_gc(p, i):
        who = (x, left, right, opp)[i]
        ref = full.at[:, who, c, :, acols(p)]
        return remote(ref, ref, s_gc.at[p, i], r_gc.at[p, i], d_mate)

    def gx_send(p):
        for way in range(2):
            copy_gx(p, way, 0).start()
        copy_gc(p, 0).start()

    def gx_forward(p):
        for way in range(2):
            copy_gx(p, way, 0).wait_recv()
            copy_gx(p, way, 1).start()
            copy_gc(p, 1 + way).start()

    def gx_last(p):
        for way in range(2):
            copy_gx(p, way, 1).wait_recv()
        copy_gc(p, 3).start()

    def g_wait(p):
        for i in range(4):
            copy_gc(p, i).wait_recv()

    for cp in locals_:
        cp.wait()
    first_rows(0)
    send_rows(1)
    second_rows(0)
    last_rows(0)
    for cp in quick:
        cp.wait_recv()
    held = jnp.zeros((8, ROWS), F32)
    for s in range(8):
        row = posb[s, pl.ds(lane, 1), :]
        held = held + jnp.where(row >= 0, F32(1.0), F32(0.0))
    count = jnp.sum(held[0:1, :])
    mate_rows(0)
    pack(0)
    factor_gram(0, 0, 2)
    first_rows(1)
    factor_gram(0, 2, 4)
    lanes = lax.broadcasted_iota(jnp.int32, (64, 128), 1)
    tops = lax.broadcasted_iota(jnp.int32, (64, 128), 0)
    for b in range(4):
        for xb in range(4):
            put = lanes == 0
            if b >= 2 and xb % 2 == 0:
                put = jnp.logical_and(put, tops > 0)
            part[b, xb, :, 512:640] = jnp.where(put, count, part[b, xb, :, 512:640])
    x_send(0, 0)
    x_send(0, 1)
    second_rows(1)
    x_relay(0)
    last_rows(1)
    mate_rows(1)
    pack(1)
    factor_gram(1, 0, 4)
    x_send(1, 0)
    x_send(1, 1)
    x_final(0)
    z_first(0)
    cross_gram(0, 2)
    z_step(0, 3)
    cross_gram(2, 4)
    z_step(0, 2)
    x_relay(1)
    x_send(2, 0)
    x_send(2, 1)
    z_step(0, 1)
    z_final(0)
    x_final(1)
    z_first(1)
    make_shard(0)
    gz_send(0, 1)
    z_step(1, 3)
    gz_wait(0, 1)
    gz_send(0, 2)
    x_relay(2)
    z_step(1, 2)
    gz_wait(0, 2)
    gz_send(0, 3)
    z_step(1, 1)
    z_final(1)
    make_shard(1)
    gz_send(1, 1)
    gz_wait(0, 3)
    gx_send(0)
    gz_wait(1, 1)
    gz_send(1, 2)
    gz_wait(1, 2)
    gz_send(1, 3)
    gz_wait(1, 3)
    gx_send(1)
    x_final(2)
    z_first(2)
    gx_forward(0)
    z_step(2, 3)
    z_step(2, 2)
    gx_forward(1)
    z_step(2, 1)
    z_final(2)
    make_shard(2)
    gz_send(2, 1)
    gx_last(0)
    gz_wait(2, 1)
    gz_send(2, 2)
    gx_last(1)
    gz_wait(2, 2)
    gz_send(2, 3)
    for cp in started:
        cp.wait_send()
    gz_wait(2, 3)
    gx_send(2)

    fac = raw_a
    row_ids = lax.broadcasted_iota(jnp.int32, (128, FEAT), 0)
    col_ids = lax.broadcasted_iota(jnp.int32, (128, FEAT), 1)
    alphas, damps = [], []
    for t in range(2):
        g_wait(t)
        first = ALL_COLS[t][0]

        def rows_of(i, first_col):
            b, h = lax.div(i, 2), lax.rem(i, 2)
            got = full[b, pl.ds(h * 2, 2), :, :, first_col]
            return got.reshape(128, 128)

        def build(i, tr, t=t, first=first):
            for k in range(8):
                j = lax.rem(i + k, 8)
                if k == 4 and t == 0:
                    i_low = lax.rem(i, 4)
                    one = rows_of(i_low, pl.ds(first + 512, 128))
                    two = rows_of(i_low + 4, pl.ds(first + 512, 128))
                    blk = jnp.where(
                        i < 4,
                        jnp.where(col_ids[:, :128] == 0, two.T, one),
                        jnp.where(row_ids[:, :128] == 0, two, one.T))
                elif k <= 4:
                    blk = rows_of(i, pl.ds(first + k * 128, 128))
                else:
                    blk = rows_of(j, pl.ds(first + (8 - k) * 128, 128)).T
                if k == 0:
                    tr = tr + jnp.sum(jnp.where(row_ids[:, :128] == col_ids[:, :128], blk, F32(0.0)))
                fac[pl.ds(pl.multiple_of(t * FEAT + i * 128, 128), 128), pl.ds(pl.multiple_of(j * 128, 128), 128)] = blk
            return tr

        trace = lax.fori_loop(0, 8, build, F32(0.0))
        damp = F32(0.1) * trace / F32(FEAT)

        def shift(i, best, t=t, damp=damp, row=0, col=t * FEAT, skip=0):
            at = pl.ds(pl.multiple_of(row + (i - skip) * 128, 128), 128)
            m = fac[pl.ds(pl.multiple_of(t * FEAT + i * 128, 128), 128), :] + jnp.where(
                row_ids + i * 128 == col_ids, damp, F32(0.0))
            hi, lo = split(m)
            pkh[at, col:col + FEAT] = hi
            pkl[at, col:col + FEAT] = lo
            return jnp.maximum(best, jnp.max(jnp.sum(jnp.abs(m), axis=1, keepdims=True)))

        best = lax.fori_loop(0, 6, shift, F32(0.0))
        best = lax.fori_loop(
            6, 8, lambda i, best, t=t: shift(i, best, row=t * 256, col=2 * FEAT, skip=6), best)
        alphas.append(F32(1.0) / jnp.full((1, 1), best, F32))
        damps.append(damp)
        if t == 0:
            gx_forward(2)
        else:
            gx_last(2)

    d = zl * 8 + x * 2 + c
    mine = pl.ds(pl.multiple_of(d * 32, 32), 32)
    mine_g = pl.ds(pl.multiple_of(FEAT + d * 32, 32), 32)
    out[0] = fac[mine, :]
    out[1] = fac[mine_g, :]

    def times(v, t):
        hi, lo = split(v)
        both = jnp.concatenate([hi, lo], axis=0)
        parts = []
        for nb in range(4):
            at = slice(t * FEAT + nb * 256, t * FEAT + nb * 256 + 256)
            low = slice(2 * FEAT + nb * 256, 2 * FEAT + nb * 256 + 256)
            end = slice(t * 256, t * 256 + 256)
            one = dot(both[:, :SLOTS], pkh[:, at]) + dot(both[:, SLOTS:], pkh[end, low])
            fine = dot(hi[:, :SLOTS], pkl[:, at]) + dot(hi[:, SLOTS:], pkl[end, low])
            parts.append(one[:32] + (one[32:] + fine))
        return jnp.concatenate(parts, axis=1)

    aa, ag = alphas
    unit_rows = jnp.where(
        lax.broadcasted_iota(jnp.int32, (32, FEAT), 0) + d * 32
        == lax.broadcasted_iota(jnp.int32, (32, FEAT), 1), F32(1.0), F32(0.0))
    shifted_rows = fac[mine_g, :] + damps[1] * unit_rows
    u1 = ag * (2.0 * unit_rows - ag * shifted_rows)
    u2 = times(u1, 1)
    inv_rows = 2.0 * u1 - ag * (2.0 * u2 - ag * times(u2, 1))
    g_wait(2)
    hi, lo = split(inv_rows)
    both = jnp.concatenate([hi, lo], axis=0)
    parts = []
    for nb in range(4):
        rh, rl = split(full[:, :, :, :, 1280 + nb * 256:1536 + nb * 256].reshape(FEAT, 256))
        one = dot(both, rh)
        parts.append(one[:32] + (one[32:] + dot(hi, rl)))
    lhs = jnp.concatenate(parts, axis=1)
    half_way = aa * (2.0 * lhs - aa * times(lhs, 0))
    w = times(half_way, 0)
    out[2] = 2.0 * half_way - aa * (2.0 * w - aa * times(w, 0))

    for p in range(3):
        for way in range(2):
            for kind in range(3):
                copy_x(p, way, kind).wait_send()
            for kind in range(5):
                k = (4, 3, 3, 2, 1)[kind]
                @pl.when(target(way, k)[1])
                def _(p=p, way=way, kind=kind):
                    copy_z(p, way, kind).wait_send()
            for step in range(1, 4):
                ok, cp = copy_gz(p, way, step)
                @pl.when(ok)
                def _(cp=cp):
                    cp.wait_send()
            for kind in range(2):
                copy_gx(p, way, kind).wait_send()
        @pl.when(home)
        def _(p=p):
            copy_c(p).wait_send()
        for i in range(4):
            copy_gc(p, i).wait_send()


def finish_kernel(got, mom, wts, out_a, out_g, out_m, out_w):
    out_a[0] = got[0]
    out_g[0] = got[1]
    moment = 0.9 * mom[0] + got[2]
    out_m[0] = moment
    out_w[0] = wts[0] - 0.5 * moment


def on_device(acts, grads_out, routes, counts, old_act_factor, old_grad_factor, momentum, weights):
    vm = pl.BlockSpec(memory_space=pltpu.VMEM)
    hbm = pl.BlockSpec(memory_space=pl.ANY)
    dma = pltpu.SemaphoreType.DMA
    got = pl.pallas_call(
        step_kernel,
        out_shape=jax.ShapeDtypeStruct((3, 32, FEAT), F32),
        in_specs=[hbm, hbm, vm, vm, vm, vm],
        out_specs=vm,
        scratch_shapes=[
            pltpu.VMEM((8 * ROWS, FEAT), F32),
            pltpu.VMEM((8 * ROWS, FEAT), F32),
            pltpu.VMEM((8, 8, ROWS), F32),
            pltpu.VMEM((SLOTS, 2 * EXT), BF16),
            pltpu.VMEM((SLOTS, 2 * EXT), BF16),
            pltpu.VMEM((4, 4, 64, SUM_W), F32),
            pltpu.VMEM((2, 4, 32, SUM_W), F32),
            pltpu.VMEM((2, 4, 32, SUM_W), F32),
            pltpu.VMEM((2, 4, 32, SUM_W), F32),
            pltpu.VMEM((32, SUM_W), F32),
            pltpu.VMEM((32, SUM_W), F32),
            pltpu.VMEM((3, 64, SUM_W), F32),
            pltpu.VMEM((3, 64, SUM_W), F32),
            pltpu.VMEM((32, SUM_W), F32),
            pltpu.VMEM((4, 4, 2, 32, ALL_W), F32),
            pltpu.VMEM((32, EXT), F32),
            dma((2,)), dma((2, 2, 2)), dma((2, 2, 2)), dma((2, 2)), dma((2, 2)),
            dma((4, 2, 2)), dma((4, 2, 2)), dma((8,)), dma((8,)),
            dma((3, 2, 3)), dma((3, 2, 3)), dma((3, 2, 5)), dma((3, 2, 5)), dma((3,)), dma((3,)),
            dma((3, 2, 3)), dma((3, 2, 3)), dma((3, 2, 2)), dma((3, 2, 2)), dma((3, 4)), dma((3, 4)),
        ],
        compiler_params=pltpu.CompilerParams(
            collective_id=0, has_side_effects=True, vmem_limit_bytes=67043328
        ),
        name="step",
    )(acts, grads_out, routes.T, counts, old_act_factor, old_grad_factor)
    out = jax.ShapeDtypeStruct((1, 32, FEAT), F32)
    return pl.pallas_call(
        finish_kernel,
        out_shape=(out, out, out, out),
        in_specs=[vm] * 3,
        out_specs=[vm] * 4,
        name="finish",
    )(got, momentum, weights)


def solution(mesh):
    rows = P(("dp", "expert"), None)
    mats = P("expert", "dp", None)
    return jax.shard_map(
        on_device,
        mesh=mesh,
        in_specs=(rows, rows, rows, rows, mats, mats, mats, mats),
        out_specs=(mats, mats, mats, mats),
        check_vma=False,
    )
```
